512 devices in a mesh: chan: 16 (over x_lo, y), ctx: 32 (over z, x_hi, core).
Axes of the slice: x: 4 (x_hi: 2, x_lo: 2; x = x_hi * 2 + x_lo), y: 8, z: 8, core: 2. Of those that a mesh axis runs over, the one named last changes fastest.
Arguments:
- gate_stream: bfloat16 [8192, 4096], P('ctx', 'chan'), may hold values from -6 to 6
- key_stream: bfloat16 [8192, 4096], P('ctx', 'chan'), may hold values from -6 to 6
- value_stream: bfloat16 [8192, 4096], P('ctx', 'chan'), may hold values from -6 to 6
- residues: float32 [16, 4096], P(None, 'chan'), may hold values from -4 to 4
- decay_rates: float32 [16, 4096], P(None, 'chan'), may hold values from 2.4414062e-06 to 0.05
- out_weight: bfloat16 [4096, 4096], P('chan'), may hold values from -0.125 to 0.125
Outputs:
- projected: bfloat16 [8192, 4096], P('ctx', 'chan')
The draws below stay inside these ranges and needn't reach their ends.
All inputs are finite; a program needn't handle non-finite values.
Results may differ from the reference program's by a relative error of at most 0.006.
Values sent between devices are 32-bit elements; how exact they have to be, the bound alone decides.
No kernel may reach another device: no remote copies, remote signals or barrier semaphores. Data moves between devices by JAX's collectives and lax.ppermute only.
A program may use at most 64 MiB of HBM per device.

```python
import math
import jax
import jax.numpy as jnp
from jax import lax

CH = 4096
ORDER = 16
SEQ = 8192


def raised(result, rng, source, target, blocks, factor):
    owner, partner = [(jnp.arange(result.shape[position]) // (result.shape[position] // blocks)).reshape([-1 if axis == position else 1 for axis in range(result.ndim)]) for position in (source, target)]
    chosen = jax.random.permutation(rng, blocks)[partner]
    strong = (owner == chosen) | (owner == (partner + blocks // 2) % blocks)
    return jnp.where(strong, factor * result, result)


def block_levels(key, extent, split, smallest, largest):
    def one(dim, parts):
        draws = jax.random.uniform(jax.random.fold_in(jax.random.fold_in(key, 6), dim), (parts,), jnp.float32, smallest / len(split), largest / len(split))
        return jnp.repeat(jnp.exp(draws), extent[dim] // parts).reshape((-1,) + (1,) * (len(extent) - dim - 1))

    level = one(*split[0])
    for cut in split[1:]:
        level = level * one(*cut)
    return level


def bell_draw(stream_key, extent, spread, limit, pieces=(), kind=jnp.bfloat16):
    gain = block_levels(stream_key, extent, pieces, -0.22, 0.18) if pieces else 1.0
    values = jax.random.normal(stream_key, extent, jnp.float32) * spread * gain
    return jnp.minimum(jnp.maximum(values, -limit), limit).astype(kind)


def noise_with(rng, dims, deviation, bound, cuts, heavy, kind=jnp.bfloat16):
    entries = deviation * jax.random.normal(rng, dims, jnp.float32)
    if cuts:
        entries = entries * block_levels(rng, dims, cuts, -0.22, 0.18)
    return jnp.clip(raised(entries, jax.random.fold_in(rng, 3), *heavy), -bound, bound).astype(kind)


def setup_inputs(seed: int = 0) -> dict:
    splits = jax.random.split(jax.random.key(seed), 7)
    gate_stream = bell_draw(splits[0], (SEQ, CH), 1.0, 6.0, ((0, 32), (1, 16)))
    key_stream = bell_draw(splits[1], (SEQ, CH), 1.0, 6.0, ((0, 32), (1, 16)))
    value_stream = bell_draw(splits[2], (SEQ, CH), 1.0, 6.0, ((0, 32), (1, 16)))
    residues = bell_draw(splits[3], (ORDER, CH), 0.25, 4.0, ((1, 16),), jnp.float32)
    decay_rates = jnp.clip(jnp.exp(math.log(0.05) - 9.927204 * jax.random.uniform(splits[4], (ORDER, CH), jnp.float32) ** block_levels(splits[4], (ORDER, CH), ((1, 16),), -0.2, 0.2)), 2.441406195430318e-06, 0.05)
    out_weight = noise_with(splits[5], (CH, CH), CH ** -0.5, 0.125, ((0, 16),), (0, 1, 16, 2.0))
    return dict(gate_stream=gate_stream, key_stream=key_stream, value_stream=value_stream, residues=residues, decay_rates=decay_rates, out_weight=out_weight)


def convolve_block(operands):
    mixed_blk, resid_blk, decay_blk = operands
    steps_t = jnp.arange(SEQ, dtype=jnp.float32)[:, None, None]
    scale = resid_blk * jnp.sqrt(-jnp.expm1(-2.0 * decay_blk))
    filt = lax.optimization_barrier(jnp.sum(scale[None] * jnp.exp(-decay_blk[None] * steps_t), axis=1))
    total = 2 * SEQ
    mixed_f = jnp.fft.rfft(mixed_blk, n=total, axis=0)
    filt_f = jnp.fft.rfft(filt, n=total, axis=0)
    return jnp.fft.irfft(mixed_f * filt_f, n=total, axis=0)[:SEQ]

def reference(gate_stream, key_stream, value_stream, residues, decay_rates, out_weight):
    block = min(256, CH)
    count = CH // block
    mixed = key_stream.astype(jnp.float32) * value_stream.astype(jnp.float32)
    mixed_blocks = jnp.transpose(mixed.reshape(SEQ, count, block), (1, 0, 2))
    resid_blocks = jnp.transpose(residues.reshape(ORDER, count, block), (1, 0, 2))
    decay_blocks = jnp.transpose(decay_rates.reshape(ORDER, count, block), (1, 0, 2))
    conv = lax.map(convolve_block, (mixed_blocks, resid_blocks, decay_blocks))
    conv = jnp.transpose(conv, (1, 0, 2)).reshape(SEQ, CH)
    gated = (gate_stream.astype(jnp.float32) * conv).astype(jnp.bfloat16)
    return jnp.dot(gated, out_weight, preferred_element_type=jnp.float32).astype(jnp.bfloat16)
```

```python
import math

import jax
import jax.numpy as jnp
from jax import lax
from jax.experimental import pallas as pl
from jax.experimental.pallas import tpu as pltpu
from jax.sharding import Mesh, PartitionSpec as P

BLOCK = 64
LANES = 128
SUB = 8


def whole(shape):
    return pl.BlockSpec(shape, lambda *_: (0,) * len(shape))


def minus_expm1(x):
    series = 1.0 - x / 8.0
    for k in (7.0, 6.0, 5.0, 4.0, 3.0, 2.0):
        series = 1.0 - x / k * series
    return jnp.where(x < 0.5, x * series, 1.0 - jnp.exp(-x))


def sub_iota():
    return lax.broadcasted_iota(jnp.int32, (SUB, LANES), 0)


def state_kernel(key_ref, value_ref, decay_ref, blocks_ref, total_ref):
    modes = decay_ref.shape[0]
    count = key_ref.shape[0] // BLOCK
    tiles = BLOCK // SUB
    back = (SUB - 1 - sub_iota()).astype(jnp.float32)

    def lane_group(g, carry):
        lanes = pl.ds(pl.multiple_of(g * LANES, LANES), LANES)
        decay = decay_ref[:, lanes]
        lam8 = jnp.exp(-decay * SUB)
        step = [jnp.broadcast_to(lam8[n : n + 1], (SUB, LANES)) for n in range(modes)]
        lam_block = jnp.exp(-decay * BLOCK)
        ends = [jnp.exp(-decay[n : n + 1] * back) for n in range(modes)]
        total = jnp.zeros((modes, LANES), jnp.float32)
        for b in range(count):
            acc = [None] * modes
            for j in range(tiles):
                rows = pl.ds(b * BLOCK + j * SUB, SUB)
                mixed = key_ref[rows, lanes].astype(jnp.float32) * value_ref[
                    rows, lanes
                ].astype(jnp.float32)
                for n in range(modes):
                    acc[n] = mixed if j == 0 else acc[n] * step[n] + mixed
            rows = [
                jnp.sum(acc[n] * ends[n], axis=0, keepdims=True) for n in range(modes)
            ]
            state = jnp.concatenate(rows, axis=0)
            blocks_ref[b, :, lanes] = state
            total = total * lam_block + state
        total_ref[:, lanes] = total
        return carry

    lax.fori_loop(0, decay_ref.shape[1] // LANES, lane_group, 0)


def local_states(key_stream, value_stream, decay_rates):
    rows, chans = key_stream.shape
    modes = decay_rates.shape[0]
    return pl.pallas_call(
        state_kernel,
        out_shape=(
            jax.ShapeDtypeStruct((rows // BLOCK, modes, chans), jnp.float32),
            jax.ShapeDtypeStruct((modes, chans), jnp.float32),
        ),
        name="local_states",
    )(key_stream, value_stream, decay_rates)


def conv_kernel(
    place_ref,
    chips_ref,
    pair_ref,
    blocks_ref,
    gate_ref,
    key_ref,
    value_ref,
    residues_ref,
    decay_ref,
    out_ref,
    taps_ref,
):
    modes = decay_ref.shape[0]
    rows = key_ref.shape[0]
    count = rows // BLOCK
    tiles = BLOCK // SUB
    chip = place_ref[0]
    core = place_ref[1]
    sub = sub_iota()
    ahead = sub.astype(jnp.float32)

    def lane_group(g, carry):
        lanes = pl.ds(pl.multiple_of(g * LANES, LANES), LANES)
        decay = decay_ref[:, lanes]
        base = residues_ref[:, lanes] * jnp.sqrt(minus_expm1(2.0 * decay))
        lam_rows = jnp.exp(-decay * float(rows))
        lam_chip = jnp.exp(-decay * float(2 * rows))
        before = jnp.zeros((modes, LANES), jnp.float32)
        for j in range(chips_ref.shape[0]):
            before = jnp.where(
                j < chip, before * lam_chip + chips_ref[j, :, lanes], before
            )
        before = jnp.where(core == 0, before, before * lam_rows + pair_ref[0, :, lanes])
        lam1 = jnp.exp(-decay)
        lam8 = jnp.exp(-decay * float(SUB))
        step = [jnp.broadcast_to(lam8[n : n + 1], (SUB, LANES)) for n in range(modes)]
        within = [jnp.exp(-decay[n : n + 1] * ahead) for n in range(modes)]
        kernel = [base[n : n + 1] * within[n] for n in range(modes)]
        for j in range(tiles):
            taps_ref[pl.ds(j * SUB, SUB), :] = sum(kernel)
            if j + 1 < tiles:
                kernel = [kernel[n] * step[n] for n in range(modes)]
        scale = base * lam1
        entry = scale * before
        fade = [entry[n : n + 1] * within[n] for n in range(modes)]
        for b in range(count):
            if b:
                entry = scale * blocks_ref[b - 1, :, lanes]
                fade = [fade[n] + entry[n : n + 1] * within[n] for n in range(modes)]
            acc = []
            mixed = []
            for j in range(tiles):
                at = pl.ds(b * BLOCK + j * SUB, SUB)
                acc.append(sum(fade))
                fade = [fade[n] * step[n] for n in range(modes)]
                mixed.append(
                    key_ref[at, lanes].astype(jnp.float32)
                    * value_ref[at, lanes].astype(jnp.float32)
                )
            for r in range(SUB):
                if r == 0:
                    moved = mixed
                else:
                    rolled = [pltpu.roll(tile, r, 0) for tile in mixed]
                    moved = []
                    for j in range(tiles):
                        above = rolled[j - 1] if j else jnp.zeros_like(rolled[0])
                        moved.append(jnp.where(sub < r, above, rolled[j]))
                for q in range(tiles):
                    tap = taps_ref[pl.ds(q * SUB + r, 1), :]
                    for j in range(q, tiles):
                        acc[j] = acc[j] + tap * moved[j - q]
            for j in range(tiles):
                at = pl.ds(b * BLOCK + j * SUB, SUB)
                gated = gate_ref[at, lanes].astype(jnp.float32) * acc[j]
                out_ref[at, lanes] = gated.astype(jnp.bfloat16).astype(jnp.float32)
        return carry

    lax.fori_loop(0, decay_ref.shape[1] // LANES, lane_group, 0)


def gated_conv(place, chips, pair, blocks, gate, key, value, residues, decay):
    rows, chans = key.shape
    args = (chips, pair, blocks, gate, key, value, residues, decay)
    return pl.pallas_call(
        conv_kernel,
        out_shape=jax.ShapeDtypeStruct((rows, chans), jnp.float32),
        grid_spec=pltpu.PrefetchScalarGridSpec(
            num_scalar_prefetch=1,
            grid=(1,),
            in_specs=[whole(a.shape) for a in args],
            out_specs=whole((rows, chans)),
            scratch_shapes=[pltpu.VMEM((BLOCK, LANES), jnp.float32)],
        ),
        name="gated_conv",
    )(place, *args)


def project_kernel(place_ref, own_ref, peer_ref, wown_ref, first_ref, second_ref, out_ref):
    half = first_ref.shape[0]
    core = place_ref[1]
    here = pl.ds(pl.multiple_of(core * half, half), half)
    there = pl.ds(pl.multiple_of((1 - core) * half, half), half)

    def product(lhs, rhs):
        return jnp.dot(
            lhs.astype(jnp.bfloat16),
            rhs.astype(jnp.bfloat16),
            preferred_element_type=jnp.float32,
        )

    out_ref[...] = (
        product(own_ref[...], wown_ref[...])
        + product(peer_ref[:, here], first_ref[...])
        + product(peer_ref[:, there], second_ref[...])
    )


def project(place, own, peer, weight, first, second):
    rows, chans = own.shape
    cols = first.shape[1]
    half = first.shape[0]
    tile = 512
    steps = cols // tile
    return pl.pallas_call(
        project_kernel,
        out_shape=jax.ShapeDtypeStruct((rows, cols), jnp.float32),
        grid_spec=pltpu.PrefetchScalarGridSpec(
            num_scalar_prefetch=1,
            grid=(steps,),
            in_specs=[
                pl.BlockSpec((rows, chans), lambda i, p: (0, 0)),
                pl.BlockSpec((rows, chans), lambda i, p: (0, 0)),
                pl.BlockSpec((chans, tile), lambda i, p: (0, p[2] * steps + i)),
                pl.BlockSpec((half, tile), lambda i, p: (0, i)),
                pl.BlockSpec((half, tile), lambda i, p: (0, i)),
            ],
            out_specs=pl.BlockSpec((rows, tile), lambda i, p: (0, i)),
        ),
        name="project",
    )(place, own, peer, weight, first, second)


def on_device(gate_stream, key_stream, value_stream, residues, decay_rates, out_weight):
    swap = [(0, 1), (1, 0)]
    rows, chans = key_stream.shape
    cols = out_weight.shape[1] // 2
    side = lax.axis_index("xl")
    core = lax.axis_index("core")
    chip = lax.axis_index("z") * lax.axis_size("xh") + lax.axis_index("xh")
    place = jnp.stack([chip, core, side]).astype(jnp.int32)
    half = chans // 2
    sent = lax.dynamic_slice(
        out_weight, (core * half, (1 - side) * cols), (half, cols)
    ).astype(jnp.float32)
    first = lax.ppermute(sent, "xl", swap)
    second = lax.ppermute(first, "core", swap)

    blocks, total = local_states(key_stream, value_stream, decay_rates)
    pair = lax.all_gather(total, "core", axis=0)
    chip_state = pair[0] * jnp.exp(-decay_rates * float(rows)) + pair[1]
    chips = lax.axis_size("z") * lax.axis_size("xh")
    copies = jnp.broadcast_to(chip_state[None], (chips,) + chip_state.shape)
    states = lax.all_to_all(copies, ("z", "xh"), split_axis=0, concat_axis=0, tiled=True)
    own = gated_conv(
        place,
        states,
        pair,
        blocks,
        gate_stream,
        key_stream,
        value_stream,
        residues,
        decay_rates,
    )
    peer = lax.ppermute(own, "xl", swap)
    partial = project(place, own, peer, out_weight, first, second)
    return lax.psum_scatter(partial, "y", scatter_dimension=1, tiled=True).astype(
        jnp.bfloat16
    )


def solution(mesh):
    inner = Mesh(mesh.devices.reshape(2, 8, 8, 2, 2), ("xl", "y", "z", "xh", "core"))
    time = ("z", "xh", "core")
    chan = ("xl", "y")
    return jax.shard_map(
        on_device,
        mesh=inner,
        in_specs=(
            P(time, chan),
            P(time, chan),
            P(time, chan),
            P(None, chan),
            P(None, chan),
            P(chan, None),
        ),
        out_specs=P(time, chan),
        check_vma=False,
    )
```

```python
import math

import jax
import jax.numpy as jnp
from jax import lax
from jax.experimental import pallas as pl
from jax.experimental.pallas import tpu as pltpu
from jax.sharding import Mesh, PartitionSpec as P

BLOCK = 64
LANES = 128
SUB = 8


def whole(shape):
    return pl.BlockSpec(shape, lambda *_: (0,) * len(shape))


def minus_expm1(x):
    series = 1.0 - x / 8.0
    for k in (7.0, 6.0, 5.0, 4.0, 3.0, 2.0):
        series = 1.0 - x / k * series
    return jnp.where(x < 0.5, x * series, 1.0 - jnp.exp(-x))


def sub_iota():
    return lax.broadcasted_iota(jnp.int32, (SUB, LANES), 0)


def state_kernel(key_ref, value_ref, decay_ref, blocks_ref, total_ref):
    modes = decay_ref.shape[0]
    count = key_ref.shape[0] // BLOCK
    tiles = BLOCK // SUB
    back = (SUB - 1 - sub_iota()).astype(jnp.float32)

    def lane_group(g, carry):
        lanes = pl.ds(pl.multiple_of(g * LANES, LANES), LANES)
        decay = decay_ref[:, lanes]
        lam8 = jnp.exp(-decay * SUB)
        step = [jnp.broadcast_to(lam8[n : n + 1], (SUB, LANES)) for n in range(modes)]
        lam_block = jnp.exp(-decay * BLOCK)
        ends = [jnp.exp(-decay[n : n + 1] * back) for n in range(modes)]
        total = jnp.zeros((modes, LANES), jnp.float32)
        for b in range(count):
            acc = [None] * modes
            for j in range(tiles):
                rows = pl.ds(b * BLOCK + j * SUB, SUB)
                mixed = key_ref[rows, lanes].astype(jnp.float32) * value_ref[
                    rows, lanes
                ].astype(jnp.float32)
                for n in range(modes):
                    acc[n] = mixed if j == 0 else acc[n] * step[n] + mixed
            rows = [
                jnp.sum(acc[n] * ends[n], axis=0, keepdims=True) for n in range(modes)
            ]
            state = jnp.concatenate(rows, axis=0)
            blocks_ref[b, :, lanes] = state
            total = total * lam_block + state
        total_ref[:, lanes] = total
        return carry

    lax.fori_loop(0, decay_ref.shape[1] // LANES, lane_group, 0)


def local_states(key_stream, value_stream, decay_rates):
    rows, chans = key_stream.shape
    modes = decay_rates.shape[0]
    return pl.pallas_call(
        state_kernel,
        out_shape=(
            jax.ShapeDtypeStruct((rows // BLOCK, modes, chans), jnp.float32),
            jax.ShapeDtypeStruct((modes, chans), jnp.float32),
        ),
        name="local_states",
    )(key_stream, value_stream, decay_rates)


def conv_kernel(
    place_ref,
    chips_ref,
    pair_ref,
    blocks_ref,
    gate_ref,
    key_ref,
    value_ref,
    residues_ref,
    decay_ref,
    out_ref,
    taps_ref,
):
    modes = decay_ref.shape[0]
    rows = key_ref.shape[0]
    count = rows // BLOCK
    tiles = BLOCK // SUB
    chip = place_ref[0]
    core = place_ref[1]
    sub = sub_iota()
    ahead = sub.astype(jnp.float32)

    def lane_group(g, carry):
        lanes = pl.ds(pl.multiple_of(g * LANES, LANES), LANES)
        decay = decay_ref[:, lanes]
        base = residues_ref[:, lanes] * jnp.sqrt(minus_expm1(2.0 * decay))
        lam_rows = jnp.exp(-decay * float(rows))
        lam_chip = jnp.exp(-decay * float(2 * rows))
        before = jnp.zeros((modes, LANES), jnp.float32)
        for j in range(chips_ref.shape[0]):
            before = jnp.where(
                j < chip, before * lam_chip + chips_ref[j, :, lanes], before
            )
        before = jnp.where(core == 0, before, before * lam_rows + pair_ref[0, :, lanes])
        lam1 = jnp.exp(-decay)
        lam8 = jnp.exp(-decay * float(SUB))
        step = [jnp.broadcast_to(lam8[n : n + 1], (SUB, LANES)) for n in range(modes)]
        within = [jnp.exp(-decay[n : n + 1] * ahead) for n in range(modes)]
        kernel = [base[n : n + 1] * within[n] for n in range(modes)]
        for j in range(tiles):
            taps_ref[pl.ds(j * SUB, SUB), :] = sum(kernel)
            if j + 1 < tiles:
                kernel = [kernel[n] * step[n] for n in range(modes)]
        scale = base * lam1
        entry = scale * before
        fade = [entry[n : n + 1] * within[n] for n in range(modes)]
        for b in range(count):
            if b:
                entry = scale * blocks_ref[b - 1, :, lanes]
                fade = [fade[n] + entry[n : n + 1] * within[n] for n in range(modes)]
            acc = []
            mixed = []
            for j in range(tiles):
                at = pl.ds(b * BLOCK + j * SUB, SUB)
                acc.append(sum(fade))
                fade = [fade[n] * step[n] for n in range(modes)]
                mixed.append(
                    key_ref[at, lanes].astype(jnp.float32)
                    * value_ref[at, lanes].astype(jnp.float32)
                )
            for r in range(SUB):
                if r == 0:
                    moved = mixed
                else:
                    rolled = [pltpu.roll(tile, r, 0) for tile in mixed]
                    moved = []
                    for j in range(tiles):
                        above = rolled[j - 1] if j else jnp.zeros_like(rolled[0])
                        moved.append(jnp.where(sub < r, above, rolled[j]))
                for q in range(tiles):
                    tap = taps_ref[pl.ds(q * SUB + r, 1), :]
                    for j in range(q, tiles):
                        acc[j] = acc[j] + tap * moved[j - q]
            for j in range(tiles):
                at = pl.ds(b * BLOCK + j * SUB, SUB)
                gated = gate_ref[at, lanes].astype(jnp.float32) * acc[j]
                out_ref[at, lanes] = gated.astype(jnp.bfloat16).astype(jnp.float32)
        return carry

    lax.fori_loop(0, decay_ref.shape[1] // LANES, lane_group, 0)


def gated_conv(place, chips, pair, blocks, gate, key, value, residues, decay):
    rows, chans = key.shape
    args = (chips, pair, blocks, gate, key, value, residues, decay)
    return pl.pallas_call(
        conv_kernel,
        out_shape=jax.ShapeDtypeStruct((rows, chans), jnp.float32),
        grid_spec=pltpu.PrefetchScalarGridSpec(
            num_scalar_prefetch=1,
            grid=(1,),
            in_specs=[whole(a.shape) for a in args],
            out_specs=whole((rows, chans)),
            scratch_shapes=[pltpu.VMEM((BLOCK, LANES), jnp.float32)],
        ),
        name="gated_conv",
    )(place, *args)


def pick_kernel(place_ref, *refs):
    for d in range(3):
        out_ref = refs[12 + d]
        for h in range(4):
            out_ref[:, h * 256 : (h + 1) * 256] = refs[4 * d + h][...].astype(jnp.float32)


def picked_weights(place, weight):
    half = weight.shape[0] // 2
    tile = 256

    def spec(d, h):
        return pl.BlockSpec(
            (half, tile),
            lambda i, p: (p[1], 8 * (p[2] ^ (d >> 1)) + 2 * h + (p[3] ^ (d & 1))),
        )

    specs = [spec(d, h) for d in (1, 2, 3) for h in range(4)]
    shape = (half, 4 * tile)
    return pl.pallas_call(
        pick_kernel,
        out_shape=[jax.ShapeDtypeStruct(shape, jnp.float32)] * 3,
        grid_spec=pltpu.PrefetchScalarGridSpec(
            num_scalar_prefetch=1,
            grid=(1,),
            in_specs=specs,
            out_specs=[whole(shape)] * 3,
        ),
        name="picked_weights",
    )(place, *[weight] * 12)


def spread_kernel(pair_ref, decay_ref, out_ref, *, rows):
    state = pair_ref[0] * jnp.exp(-decay_ref[...] * float(rows)) + pair_ref[1]
    out_ref[...] = jnp.broadcast_to(state[None], out_ref.shape)


def spread_states(pair, decay_rates, rows, chips):
    return pl.pallas_call(
        lambda *refs: spread_kernel(*refs, rows=rows),
        out_shape=jax.ShapeDtypeStruct((chips,) + decay_rates.shape, jnp.float32),
        name="spread_states",
    )(pair, decay_rates)


def project_kernel(place_ref, own_ref, p1_ref, p2_ref, p3_ref, wown_ref, near_ref, far_ref, out_ref):
    half = wown_ref.shape[0] // 2
    core = place_ref[1]
    here = pl.ds(pl.multiple_of(core * half, half), half)
    there = pl.ds(pl.multiple_of((1 - core) * half, half), half)

    def product(lhs, rhs):
        return jnp.dot(
            lhs.astype(jnp.bfloat16),
            rhs.astype(jnp.bfloat16),
            preferred_element_type=jnp.float32,
        )

    acc = product(own_ref[...], wown_ref[...])
    for d, peer_ref in enumerate((p1_ref, p2_ref, p3_ref)):
        acc += product(peer_ref[:, here], near_ref[d * half : (d + 1) * half, :])
        acc += product(peer_ref[:, there], far_ref[d * half : (d + 1) * half, :])
    out_ref[0] = acc


def project(place, own, peers, weight, near, far):
    rows, chans = own.shape
    tile = chans
    gated = pl.BlockSpec((rows, chans), lambda i, p: (0, 0))
    other = pl.BlockSpec((near.shape[0], tile), lambda i, p: (0, i))
    return pl.pallas_call(
        project_kernel,
        out_shape=jax.ShapeDtypeStruct((4, rows, tile), jnp.float32),
        grid_spec=pltpu.PrefetchScalarGridSpec(
            num_scalar_prefetch=1,
            grid=(4,),
            in_specs=[gated] * 4
            + [pl.BlockSpec((chans, tile), lambda i, p: (0, 8 * p[2] + 2 * i + p[3]))]
            + [other] * 2,
            out_specs=pl.BlockSpec((1, rows, tile), lambda i, p: (i, 0, 0)),
        ),
        name="project",
    )(place, own, *peers, weight, near, far)


def on_device(gate_stream, key_stream, value_stream, residues, decay_rates, out_weight):
    rows, chans = key_stream.shape
    quad = ("xl", "yl")
    routes = [[(g, g ^ d) for g in range(4)] for d in (1, 2, 3)]
    chip = lax.axis_index("z") * lax.axis_size("xh") + lax.axis_index("xh")
    place = jnp.stack(
        [chip, lax.axis_index("core"), lax.axis_index("xl"), lax.axis_index("yl")]
    ).astype(jnp.int32)
    blocks, total = local_states(key_stream, value_stream, decay_rates)
    pair = lax.all_gather(total, "core", axis=0)
    chips = lax.axis_size("z") * lax.axis_size("xh")
    copies = spread_states(pair, decay_rates, rows, chips)
    sent = picked_weights(place, out_weight)
    *sent, copies = lax.optimization_barrier((*sent, copies))
    states = lax.all_to_all(copies, ("z", "xh"), split_axis=0, concat_axis=0, tiled=True)
    near = [lax.ppermute(s, quad, r) for s, r in zip(sent, routes)]
    *near, states = lax.optimization_barrier((*near, states))
    near = jnp.concatenate(near, axis=0)
    far = lax.ppermute(near, "core", [(0, 1), (1, 0)])
    own = gated_conv(
        place,
        states,
        pair,
        blocks,
        gate_stream,
        key_stream,
        value_stream,
        residues,
        decay_rates,
    )
    peers = [lax.ppermute(own, quad, r) for r in routes]
    partial = project(place, own, peers, out_weight, near, far)
    parts = lax.all_to_all(partial, "yh", split_axis=0, concat_axis=0, tiled=True)
    return jnp.sum(parts, axis=0).astype(jnp.bfloat16)


def solution(mesh):
    inner = Mesh(
        mesh.devices.reshape(2, 4, 2, 8, 2, 2), ("xl", "yh", "yl", "z", "xh", "core")
    )
    time = ("z", "xh", "core")
    chan = ("xl", "yh", "yl")
    return jax.shard_map(
        on_device,
        mesh=inner,
        in_specs=(
            P(time, chan),
            P(time, chan),
            P(time, chan),
            P(None, chan),
            P(None, chan),
            P(chan, None),
        ),
        out_specs=P(time, chan),
        check_vma=False,
    )
```

```python
import math

import jax
import jax.numpy as jnp
from jax import lax
from jax.experimental import pallas as pl
from jax.experimental.pallas import tpu as pltpu
from jax.sharding import Mesh, PartitionSpec as P

BLOCK = 64
LANES = 128
SUB = 8


def near_core(array):
    return pltpu.with_memory_space_constraint(array, pltpu.VMEM)


def in_hbm(*arrays):
    return [pltpu.with_memory_space_constraint(a, pltpu.HBM) for a in arrays]


def whole(shape):
    return pl.BlockSpec(shape, lambda *_: (0,) * len(shape))


def minus_expm1(x):
    series = 1.0 - x / 8.0
    for k in (7.0, 6.0, 5.0, 4.0, 3.0, 2.0):
        series = 1.0 - x / k * series
    return jnp.where(x < 0.5, x * series, 1.0 - jnp.exp(-x))


def sub_iota():
    return lax.broadcasted_iota(jnp.int32, (SUB, LANES), 0)


def state_kernel(key_ref, value_ref, decay_ref, blocks_ref, total_ref):
    modes = decay_ref.shape[0]
    count = key_ref.shape[0] // BLOCK
    tiles = BLOCK // SUB
    back = (SUB - 1 - sub_iota()).astype(jnp.float32)

    def lane_group(g, carry):
        lanes = pl.ds(pl.multiple_of(g * LANES, LANES), LANES)
        decay = decay_ref[:, lanes]
        lam8 = jnp.exp(-decay * SUB)
        step = [jnp.broadcast_to(lam8[n : n + 1], (SUB, LANES)) for n in range(modes)]
        lam_block = jnp.exp(-decay * BLOCK)
        ends = [jnp.exp(-decay[n : n + 1] * back) for n in range(modes)]
        total = jnp.zeros((modes, LANES), jnp.float32)
        for b in range(count):
            acc = [None] * modes
            for j in range(tiles):
                rows = pl.ds(b * BLOCK + j * SUB, SUB)
                mixed = key_ref[rows, lanes].astype(jnp.float32) * value_ref[
                    rows, lanes
                ].astype(jnp.float32)
                for n in range(modes):
                    acc[n] = mixed if j == 0 else acc[n] * step[n] + mixed
            rows = [
                jnp.sum(acc[n] * ends[n], axis=0, keepdims=True) for n in range(modes)
            ]
            state = jnp.concatenate(rows, axis=0)
            blocks_ref[b, :, lanes] = state
            total = total * lam_block + state
        total_ref[:, lanes] = total
        return carry

    lax.fori_loop(0, decay_ref.shape[1] // LANES, lane_group, 0)


def local_states(key_stream, value_stream, decay_rates):
    rows, chans = key_stream.shape
    modes = decay_rates.shape[0]
    return pl.pallas_call(
        state_kernel,
        out_shape=(
            jax.ShapeDtypeStruct((rows // BLOCK, modes, chans), jnp.float32),
            jax.ShapeDtypeStruct((modes, chans), jnp.float32),
        ),
        name="local_states",
    )(key_stream, value_stream, decay_rates)


def conv_kernel(
    place_ref,
    chips_ref,
    pair_ref,
    blocks_ref,
    gate_ref,
    key_ref,
    value_ref,
    residues_ref,
    decay_ref,
    out_ref,
    taps_ref,
):
    modes = decay_ref.shape[0]
    rows = key_ref.shape[0]
    count = rows // BLOCK
    tiles = BLOCK // SUB
    chip = place_ref[0]
    core = place_ref[1]
    sub = sub_iota()
    ahead = sub.astype(jnp.float32)

    def lane_group(g, carry):
        lanes = pl.ds(pl.multiple_of(g * LANES, LANES), LANES)
        decay = decay_ref[:, lanes]
        base = residues_ref[:, lanes] * jnp.sqrt(minus_expm1(2.0 * decay))
        lam_rows = jnp.exp(-decay * float(rows))
        lam_chip = jnp.exp(-decay * float(2 * rows))
        before = jnp.zeros((modes, LANES), jnp.float32)
        for j in range(chips_ref.shape[0]):
            before = jnp.where(
                j < chip, before * lam_chip + chips_ref[j, :, lanes], before
            )
        before = jnp.where(core == 0, before, before * lam_rows + pair_ref[0, :, lanes])
        lam1 = jnp.exp(-decay)
        lam8 = jnp.exp(-decay * float(SUB))
        step = [jnp.broadcast_to(lam8[n : n + 1], (SUB, LANES)) for n in range(modes)]
        within = [jnp.exp(-decay[n : n + 1] * ahead) for n in range(modes)]
        kernel = [base[n : n + 1] * within[n] for n in range(modes)]
        for j in range(tiles):
            taps_ref[pl.ds(j * SUB, SUB), :] = sum(kernel)
            if j + 1 < tiles:
                kernel = [kernel[n] * step[n] for n in range(modes)]
        scale = base * lam1
        entry = scale * before
        fade = [entry[n : n + 1] * within[n] for n in range(modes)]
        for b in range(count):
            if b:
                entry = scale * blocks_ref[b - 1, :, lanes]
                fade = [fade[n] + entry[n : n + 1] * within[n] for n in range(modes)]
            acc = []
            mixed = []
            for j in range(tiles):
                at = pl.ds(b * BLOCK + j * SUB, SUB)
                acc.append(sum(fade))
                fade = [fade[n] * step[n] for n in range(modes)]
                mixed.append(
                    key_ref[at, lanes].astype(jnp.float32)
                    * value_ref[at, lanes].astype(jnp.float32)
                )
            for r in range(SUB):
                if r == 0:
                    moved = mixed
                else:
                    rolled = [pltpu.roll(tile, r, 0) for tile in mixed]
                    moved = []
                    for j in range(tiles):
                        above = rolled[j - 1] if j else jnp.zeros_like(rolled[0])
                        moved.append(jnp.where(sub < r, above, rolled[j]))
                for q in range(tiles):
                    tap = taps_ref[pl.ds(q * SUB + r, 1), :]
                    for j in range(q, tiles):
                        acc[j] = acc[j] + tap * moved[j - q]
            for j in range(tiles):
                at = pl.ds(b * BLOCK + j * SUB, SUB)
                gated = gate_ref[at, lanes].astype(jnp.float32) * acc[j]
                out_ref[at, lanes] = gated.astype(jnp.bfloat16).astype(jnp.float32)
        return carry

    lax.fori_loop(0, decay_ref.shape[1] // LANES, lane_group, 0)


def gated_conv(place, chips, pair, blocks, gate, key, value, residues, decay):
    rows, chans = key.shape
    args = (near_core(chips), pair, blocks, gate, key, value, residues, decay)
    return pl.pallas_call(
        conv_kernel,
        out_shape=jax.ShapeDtypeStruct((rows, chans), jnp.float32),
        grid_spec=pltpu.PrefetchScalarGridSpec(
            num_scalar_prefetch=1,
            grid=(1,),
            in_specs=[whole(a.shape) for a in args],
            out_specs=whole((rows, chans)),
            scratch_shapes=[pltpu.VMEM((BLOCK, LANES), jnp.float32)],
        ),
        cost_estimate=pl.CostEstimate(
            flops=2 * 10**11, transcendentals=0, bytes_accessed=2 * 10**8
        ),
        name="gated_conv",
    )(place, *args)


def pick_kernel(place_ref, *refs):
    for d in range(3):
        out_ref = refs[12 + d]
        for h in range(4):
            out_ref[:, h * 256 : (h + 1) * 256] = refs[4 * d + h][...].astype(jnp.float32)


def picked_weights(place, weight):
    half = weight.shape[0] // 2
    tile = 256

    def spec(d, h):
        return pl.BlockSpec(
            (half, tile),
            lambda i, p: (p[1], 8 * (p[2] ^ (d >> 1)) + 2 * h + (p[3] ^ (d & 1))),
        )

    specs = [spec(d, h) for d in (1, 2, 3) for h in range(4)]
    shape = (half, 4 * tile)
    return pl.pallas_call(
        pick_kernel,
        out_shape=[jax.ShapeDtypeStruct(shape, jnp.float32)] * 3,
        grid_spec=pltpu.PrefetchScalarGridSpec(
            num_scalar_prefetch=1,
            grid=(1,),
            in_specs=specs,
            out_specs=[whole(shape)] * 3,
        ),
        name="picked_weights",
    )(place, *[weight] * 12)


def spread_kernel(pair_ref, decay_ref, out_ref, *, rows):
    state = pair_ref[0] * jnp.exp(-decay_ref[...] * float(rows)) + pair_ref[1]
    out_ref[...] = jnp.broadcast_to(state[None], out_ref.shape)


def spread_states(pair, decay_rates, rows, chips):
    return pl.pallas_call(
        lambda *refs: spread_kernel(*refs, rows=rows),
        out_shape=jax.ShapeDtypeStruct((chips,) + decay_rates.shape, jnp.float32),
        name="spread_states",
    )(pair, decay_rates)


def weights_kernel(place_ref, wown_ref, near_ref, far_ref, out_ref):
    half = wown_ref.shape[0] // 2
    core = place_ref[1]
    out_ref[: 2 * half, :] = wown_ref[...]
    for d in range(3):
        top = 2 * half * (d + 1)
        part = pl.ds(d * half, half)
        here = pl.ds(pl.multiple_of(top + core * half, half), half)
        there = pl.ds(pl.multiple_of(top + (1 - core) * half, half), half)
        out_ref[here, :] = near_ref[part, :].astype(jnp.bfloat16)
        out_ref[there, :] = far_ref[part, :].astype(jnp.bfloat16)


def joined_weights(place, weight, near, far):
    chans = weight.shape[0]
    other = pl.BlockSpec((near.shape[0], chans), lambda i, p: (0, i))
    return pl.pallas_call(
        weights_kernel,
        out_shape=jax.ShapeDtypeStruct((4 * chans, 4 * chans), jnp.bfloat16),
        grid_spec=pltpu.PrefetchScalarGridSpec(
            num_scalar_prefetch=1,
            grid=(4,),
            in_specs=[
                pl.BlockSpec((chans, chans), lambda i, p: (0, 8 * p[2] + 2 * i + p[3])),
                other,
                other,
            ],
            out_specs=pl.BlockSpec((4 * chans, chans), lambda i, p: (0, i)),
        ),
        cost_estimate=pl.CostEstimate(flops=1000, transcendentals=0, bytes_accessed=1000),
        name="joined_weights",
    )(place, weight, *in_hbm(near, far))


def project_kernel(own_ref, p1_ref, p2_ref, p3_ref, weight_ref, out_ref):
    chans = own_ref.shape[1]
    acc = None
    for d, ref in enumerate((own_ref, p1_ref, p2_ref, p3_ref)):
        term = jnp.dot(
            ref[...].astype(jnp.bfloat16),
            weight_ref[d * chans : (d + 1) * chans, :],
            preferred_element_type=jnp.float32,
        )
        acc = term if acc is None else acc + term
    out_ref[0] = acc


def project(own, peers, weight):
    rows, chans = own.shape
    return pl.pallas_call(
        project_kernel,
        out_shape=jax.ShapeDtypeStruct((4, rows, chans), jnp.float32),
        grid=(4,),
        in_specs=[pl.BlockSpec((rows, chans), lambda i: (0, 0))] * 4
        + [pl.BlockSpec((4 * chans, chans), lambda i: (0, i))],
        out_specs=pl.BlockSpec((1, rows, chans), lambda i: (i, 0, 0)),
        name="project",
    )(*in_hbm(own, *peers), weight)


def on_device(gate_stream, key_stream, value_stream, residues, decay_rates, out_weight):
    rows, chans = key_stream.shape
    quad = ("xl", "yl")
    routes = [[(g, g ^ d) for g in range(4)] for d in (1, 2, 3)]
    chip = lax.axis_index("z") * lax.axis_size("xh") + lax.axis_index("xh")
    place = jnp.stack(
        [chip, lax.axis_index("core"), lax.axis_index("xl"), lax.axis_index("yl")]
    ).astype(jnp.int32)
    blocks, total = local_states(key_stream, value_stream, decay_rates)
    pair = lax.all_gather(total, "core", axis=0)
    chips = lax.axis_size("z") * lax.axis_size("xh")
    copies = spread_states(pair, decay_rates, rows, chips)
    sent = picked_weights(place, out_weight)
    states = lax.all_to_all(copies, ("z", "xh"), split_axis=0, concat_axis=0, tiled=True)
    near = [lax.ppermute(s, quad, r) for s, r in zip(sent, routes)]
    own = gated_conv(
        place,
        states,
        pair,
        blocks,
        gate_stream,
        key_stream,
        value_stream,
        residues,
        decay_rates,
    )
    peers = [lax.ppermute(own, quad, r) for r in routes]
    near = jnp.concatenate(near, axis=0)
    near, _ = lax.optimization_barrier((near, peers[2]))
    far = lax.ppermute(near, "core", [(0, 1), (1, 0)])
    weight = joined_weights(place, out_weight, near, far)
    partial = project(own, peers, weight)
    parts = lax.all_to_all(partial, "yh", split_axis=0, concat_axis=0, tiled=True)
    return jnp.sum(parts, axis=0).astype(jnp.bfloat16)


def solution(mesh):
    inner = Mesh(
        mesh.devices.reshape(2, 4, 2, 8, 2, 2), ("xl", "yh", "yl", "z", "xh", "core")
    )
    time = ("z", "xh", "core")
    chan = ("xl", "yh", "yl")
    return jax.shard_map(
        on_device,
        mesh=inner,
        in_specs=(
            P(time, chan),
            P(time, chan),
            P(time, chan),
            P(None, chan),
            P(None, chan),
            P(chan, None),
        ),
        out_specs=P(time, chan),
        check_vma=False,
    )
```

```python
import math

import jax
import jax.numpy as jnp
from jax import lax
from jax.experimental import pallas as pl
from jax.experimental.pallas import tpu as pltpu
from jax.sharding import Mesh, PartitionSpec as P

BLOCK = 64
LANES = 128
SUB = 8


def near_core(array):
    return pltpu.with_memory_space_constraint(array, pltpu.VMEM)


def in_hbm(*arrays):
    return [pltpu.with_memory_space_constraint(a, pltpu.HBM) for a in arrays]


def whole(shape):
    return pl.BlockSpec(shape, lambda *_: (0,) * len(shape))


def minus_expm1(x):
    series = 1.0 - x / 8.0
    for k in (7.0, 6.0, 5.0, 4.0, 3.0, 2.0):
        series = 1.0 - x / k * series
    return jnp.where(x < 0.5, x * series, 1.0 - jnp.exp(-x))


def sub_iota():
    return lax.broadcasted_iota(jnp.int32, (SUB, LANES), 0)


def state_kernel(key_ref, value_ref, decay_ref, blocks_ref, total_ref):
    modes = decay_ref.shape[0]
    count = key_ref.shape[0] // BLOCK
    tiles = BLOCK // SUB
    back = (SUB - 1 - sub_iota()).astype(jnp.float32)

    def lane_group(g, carry):
        lanes = pl.ds(pl.multiple_of(g * LANES, LANES), LANES)
        decay = decay_ref[:, lanes]
        lam8 = jnp.exp(-decay * SUB)
        step = [jnp.broadcast_to(lam8[n : n + 1], (SUB, LANES)) for n in range(modes)]
        lam_block = jnp.exp(-decay * BLOCK)
        ends = [jnp.exp(-decay[n : n + 1] * back) for n in range(modes)]
        total = jnp.zeros((modes, LANES), jnp.float32)
        for b in range(count):
            acc = [None] * modes
            for j in range(tiles):
                rows = pl.ds(b * BLOCK + j * SUB, SUB)
                mixed = key_ref[rows, lanes].astype(jnp.float32) * value_ref[
                    rows, lanes
                ].astype(jnp.float32)
                for n in range(modes):
                    acc[n] = mixed if j == 0 else acc[n] * step[n] + mixed
            rows = [
                jnp.sum(acc[n] * ends[n], axis=0, keepdims=True) for n in range(modes)
            ]
            state = jnp.concatenate(rows, axis=0)
            blocks_ref[b, :, lanes] = state
            total = total * lam_block + state
        total_ref[:, lanes] = total
        return carry

    lax.fori_loop(0, decay_ref.shape[1] // LANES, lane_group, 0)


def local_states(key_stream, value_stream, decay_rates):
    rows, chans = key_stream.shape
    modes = decay_rates.shape[0]
    return pl.pallas_call(
        state_kernel,
        out_shape=(
            jax.ShapeDtypeStruct((rows // BLOCK, modes, chans), jnp.float32),
            jax.ShapeDtypeStruct((modes, chans), jnp.float32),
        ),
        name="local_states",
    )(key_stream, value_stream, decay_rates)


def conv_kernel(
    place_ref,
    chips_ref,
    pair_ref,
    blocks_ref,
    gate_ref,
    key_ref,
    value_ref,
    residues_ref,
    decay_ref,
    out_ref,
    taps_ref,
):
    modes = decay_ref.shape[0]
    rows = key_ref.shape[0]
    count = rows // BLOCK
    tiles = BLOCK // SUB
    chip = place_ref[0]
    core = place_ref[1]
    sub = sub_iota()
    ahead = sub.astype(jnp.float32)

    def lane_group(g, carry):
        lanes = pl.ds(pl.multiple_of(g * LANES, LANES), LANES)
        decay = decay_ref[:, lanes]
        base = residues_ref[:, lanes] * jnp.sqrt(minus_expm1(2.0 * decay))
        lam_rows = jnp.exp(-decay * float(rows))
        lam_chip = jnp.exp(-decay * float(2 * rows))
        before = jnp.zeros((modes, LANES), jnp.float32)
        for j in range(chips_ref.shape[0]):
            before = jnp.where(
                j < chip, before * lam_chip + chips_ref[j, :, lanes], before
            )
        before = jnp.where(core == 0, before, before * lam_rows + pair_ref[0, :, lanes])
        lam1 = jnp.exp(-decay)
        lam8 = jnp.exp(-decay * float(SUB))
        step = [jnp.broadcast_to(lam8[n : n + 1], (SUB, LANES)) for n in range(modes)]
        within = [jnp.exp(-decay[n : n + 1] * ahead) for n in range(modes)]
        kernel = [base[n : n + 1] * within[n] for n in range(modes)]
        for j in range(tiles):
            taps_ref[pl.ds(j * SUB, SUB), :] = sum(kernel)
            if j + 1 < tiles:
                kernel = [kernel[n] * step[n] for n in range(modes)]
        scale = base * lam1
        entry = scale * before
        fade = [entry[n : n + 1] * within[n] for n in range(modes)]
        for b in range(count):
            if b:
                entry = scale * blocks_ref[b - 1, :, lanes]
                fade = [fade[n] + entry[n : n + 1] * within[n] for n in range(modes)]
            acc = []
            mixed = []
            for j in range(tiles):
                at = pl.ds(b * BLOCK + j * SUB, SUB)
                acc.append(sum(fade))
                fade = [fade[n] * step[n] for n in range(modes)]
                mixed.append(
                    key_ref[at, lanes].astype(jnp.float32)
                    * value_ref[at, lanes].astype(jnp.float32)
                )
            for r in range(SUB):
                if r == 0:
                    moved = mixed
                else:
                    rolled = [pltpu.roll(tile, r, 0) for tile in mixed]
                    moved = []
                    for j in range(tiles):
                        above = rolled[j - 1] if j else jnp.zeros_like(rolled[0])
                        moved.append(jnp.where(sub < r, above, rolled[j]))
                for q in range(tiles):
                    tap = taps_ref[pl.ds(q * SUB + r, 1), :]
                    for j in range(q, tiles):
                        acc[j] = acc[j] + tap * moved[j - q]
            for j in range(tiles):
                at = pl.ds(b * BLOCK + j * SUB, SUB)
                gated = gate_ref[at, lanes].astype(jnp.float32) * acc[j]
                out_ref[at, lanes] = gated.astype(jnp.bfloat16).astype(jnp.float32)
        return carry

    lax.fori_loop(0, decay_ref.shape[1] // LANES, lane_group, 0)


def gated_conv(place, chips, pair, blocks, gate, key, value, residues, decay):
    rows, chans = key.shape
    args = (near_core(chips), pair, blocks, gate, key, value, residues, decay)
    return pl.pallas_call(
        conv_kernel,
        out_shape=jax.ShapeDtypeStruct((rows, chans), jnp.float32),
        grid_spec=pltpu.PrefetchScalarGridSpec(
            num_scalar_prefetch=1,
            grid=(1,),
            in_specs=[whole(a.shape) for a in args],
            out_specs=whole((rows, chans)),
            scratch_shapes=[pltpu.VMEM((BLOCK, LANES), jnp.float32)],
        ),
        cost_estimate=pl.CostEstimate(
            flops=2 * 10**11, transcendentals=0, bytes_accessed=2 * 10**8
        ),
        name="gated_conv",
    )(place, *args)


def pick_kernel(place_ref, weight_ref, out_ref):
    out_ref[...] = weight_ref[...].astype(jnp.float32)


def picked_weights(place, weight):
    half = weight.shape[0] // 2
    cols = weight.shape[1] // 2
    return pl.pallas_call(
        pick_kernel,
        out_shape=jax.ShapeDtypeStruct((half, cols), jnp.float32),
        grid_spec=pltpu.PrefetchScalarGridSpec(
            num_scalar_prefetch=1,
            grid=(1,),
            in_specs=[pl.BlockSpec((half, cols), lambda i, p: (p[1], 1 - p[2]))],
            out_specs=whole((half, cols)),
        ),
        name="picked_weights",
    )(place, weight)


def spread_kernel(pair_ref, decay_ref, out_ref, *, rows):
    state = pair_ref[0] * jnp.exp(-decay_ref[...] * float(rows)) + pair_ref[1]
    out_ref[...] = jnp.broadcast_to(state[None], out_ref.shape)


def spread_states(pair, decay_rates, rows, chips):
    return pl.pallas_call(
        lambda *refs: spread_kernel(*refs, rows=rows),
        out_shape=jax.ShapeDtypeStruct((chips,) + decay_rates.shape, jnp.float32),
        name="spread_states",
    )(pair, decay_rates)


def weights_kernel(place_ref, own_ref, near_ref, far_ref, out_ref):
    half = near_ref.shape[0]
    chans = 2 * half
    core = place_ref[1]
    parity = place_ref[3]
    here = pl.ds(pl.multiple_of(chans + core * half, half), half)
    there = pl.ds(pl.multiple_of(chans + (1 - core) * half, half), half)
    for h in range(4):
        for kept in range(2):
            side = parity if kept else 1 - parity
            source = pl.ds(pl.multiple_of((2 * h + side) * chans, chans), chans)
            target = slice((4 * kept + h) * chans, (4 * kept + h + 1) * chans)
            out_ref[:chans, target] = own_ref[:, source]
            out_ref[here, target] = near_ref[:, source].astype(jnp.bfloat16)
            out_ref[there, target] = far_ref[:, source].astype(jnp.bfloat16)


def joined_weights(place, weight, near, far):
    chans = weight.shape[0]
    half, cols = near.shape
    return pl.pallas_call(
        weights_kernel,
        out_shape=jax.ShapeDtypeStruct((2 * chans, cols), jnp.bfloat16),
        grid_spec=pltpu.PrefetchScalarGridSpec(
            num_scalar_prefetch=1,
            grid=(1,),
            in_specs=[
                pl.BlockSpec((chans, cols), lambda i, p: (0, p[2])),
                whole((half, cols)),
                whole((half, cols)),
            ],
            out_specs=whole((2 * chans, cols)),
        ),
        name="joined_weights",
    )(place, weight, near, far)


def project_kernel(own_ref, peer_ref, weight_ref, out_ref):
    chans = own_ref.shape[1]
    gated = jnp.concatenate([own_ref[...], peer_ref[...]], axis=1).astype(jnp.bfloat16)
    for h in range(4):
        out_ref[h] = jnp.dot(
            gated,
            weight_ref[:, h * chans : (h + 1) * chans],
            preferred_element_type=jnp.float32,
        )


def project(own, peer, weight, part, name):
    rows, chans = own.shape
    return pl.pallas_call(
        project_kernel,
        out_shape=jax.ShapeDtypeStruct((4, rows, chans), jnp.float32),
        grid=(1,),
        in_specs=[
            whole((rows, chans)),
            whole((rows, chans)),
            pl.BlockSpec((2 * chans, 4 * chans), lambda i: (0, part)),
        ],
        out_specs=whole((4, rows, chans)),
        name=name,
    )(own, peer, weight)


def neighbour_routes(count):
    routes = []
    for y in range(count):
        routes.append((2 * y, 2 * (y ^ 1)))
        other = (y + 1) % count if y % 2 else (y - 1) % count
        routes.append((2 * y + 1, 2 * other + 1))
    return routes


def weight_routes():
    routes = []
    for side in range(2):
        for xh in range(2):
            for core in range(2):
                source = 4 * side + 2 * xh + core
                routes.append((source, 4 * (1 - side) + 2 * (xh ^ core) + core))
    return routes


def on_device(gate_stream, key_stream, value_stream, residues, decay_rates, out_weight):
    rows, chans = key_stream.shape
    swap = [(0, 1), (1, 0)]
    chip = lax.axis_index("z") * lax.axis_size("xh") + lax.axis_index("xh")
    place = jnp.stack(
        [chip, lax.axis_index("core"), lax.axis_index("xl"), lax.axis_index("yl")]
    ).astype(jnp.int32)
    blocks, total = local_states(key_stream, value_stream, decay_rates)
    pair = lax.all_gather(total, "core", axis=0)
    chips = lax.axis_size("z") * lax.axis_size("xh")
    copies = spread_states(pair, decay_rates, rows, chips)
    states = lax.all_to_all(copies, ("z", "xh"), split_axis=0, concat_axis=0, tiled=True)
    sent = picked_weights(place, out_weight)
    near = lax.ppermute(sent, ("xl", "xh", "core"), weight_routes())
    far = lax.ppermute(near, "core", swap)
    weight = joined_weights(place, out_weight, near, far)
    own = gated_conv(
        place,
        states,
        pair,
        blocks,
        gate_stream,
        key_stream,
        value_stream,
        residues,
        decay_rates,
    )
    peer = lax.ppermute(own, "xl", swap)
    leaving = project(own, peer, weight, 0, "project_leaving")
    arrived = lax.ppermute(leaving, ("yh", "yl", "core"), neighbour_routes(8))
    kept = project(own, peer, weight, 1, "project_kept")
    parts = lax.all_to_all(kept + arrived, "yh", split_axis=0, concat_axis=0, tiled=True)
    return jnp.sum(parts, axis=0).astype(jnp.bfloat16)


def solution(mesh):
    inner = Mesh(
        mesh.devices.reshape(2, 4, 2, 8, 2, 2), ("xl", "yh", "yl", "z", "xh", "core")
    )
    time = ("z", "xh", "core")
    chan = ("xl", "yh", "yl")
    return jax.shard_map(
        on_device,
        mesh=inner,
        in_specs=(
            P(time, chan),
            P(time, chan),
            P(time, chan),
            P(None, chan),
            P(None, chan),
            P(chan, None),
        ),
        out_specs=P(time, chan),
        check_vma=False,
    )
```

```python
import functools

import jax
import jax.numpy as jnp
from jax import lax
from jax.experimental import pallas as pl
from jax.experimental.pallas import tpu as pltpu
from jax.sharding import Mesh, PartitionSpec as P

BLOCK = 64
LANES = 128
SUB = 8


def near_core(array):
    return pltpu.with_memory_space_constraint(array, pltpu.VMEM)


def whole(shape):
    return pl.BlockSpec(shape, lambda *_: (0,) * len(shape))


def minus_expm1(x):
    series = 1.0 - x / 8.0
    for k in (7.0, 6.0, 5.0, 4.0, 3.0, 2.0):
        series = 1.0 - x / k * series
    return jnp.where(x < 0.5, x * series, 1.0 - jnp.exp(-x))


def sub_iota():
    return lax.broadcasted_iota(jnp.int32, (SUB, LANES), 0)


def state_kernel(key_ref, value_ref, decay_ref, blocks_ref, copies_ref):
    modes = decay_ref.shape[0]
    count = key_ref.shape[0] // BLOCK
    tiles = BLOCK // SUB
    back = (SUB - 1 - sub_iota()).astype(jnp.float32)

    def lane_group(g, carry):
        lanes = pl.ds(pl.multiple_of(g * LANES, LANES), LANES)
        decay = decay_ref[:, lanes]
        lam8 = jnp.exp(-decay * SUB)
        step = [jnp.broadcast_to(lam8[n : n + 1], (SUB, LANES)) for n in range(modes)]
        lam_block = jnp.exp(-decay * BLOCK)
        ends = [jnp.exp(-decay[n : n + 1] * back) for n in range(modes)]
        total = jnp.zeros((modes, LANES), jnp.float32)
        for b in range(count):
            acc = [None] * modes
            for j in range(tiles):
                rows = pl.ds(b * BLOCK + j * SUB, SUB)
                mixed = key_ref[rows, lanes].astype(jnp.float32) * value_ref[
                    rows, lanes
                ].astype(jnp.float32)
                for n in range(modes):
                    acc[n] = mixed if j == 0 else acc[n] * step[n] + mixed
            rows = [
                jnp.sum(acc[n] * ends[n], axis=0, keepdims=True) for n in range(modes)
            ]
            state = jnp.concatenate(rows, axis=0)
            blocks_ref[b, :, lanes] = state
            total = total * lam_block + state
        for j in range(copies_ref.shape[0]):
            copies_ref[j, :, lanes] = total
        return carry

    lax.fori_loop(0, decay_ref.shape[1] // LANES, lane_group, 0)


def local_states(key_stream, value_stream, decay_rates, chips):
    rows, chans = key_stream.shape
    modes = decay_rates.shape[0]
    return pl.pallas_call(
        state_kernel,
        out_shape=(
            jax.ShapeDtypeStruct((rows // BLOCK, modes, chans), jnp.float32),
            jax.ShapeDtypeStruct((chips, modes, chans), jnp.float32),
        ),
        name="local_states",
    )(key_stream, value_stream, decay_rates)


def local_kernel(
    blocks_ref, gate_ref, key_ref, value_ref, residues_ref, decay_ref, out_ref, taps_ref
):
    modes = decay_ref.shape[0]
    rows = key_ref.shape[0]
    count = rows // BLOCK
    tiles = BLOCK // SUB
    sub = sub_iota()
    ahead = sub.astype(jnp.float32)

    def lane_group(g, carry):
        lanes = pl.ds(pl.multiple_of(g * LANES, LANES), LANES)
        decay = decay_ref[:, lanes]
        base = residues_ref[:, lanes] * jnp.sqrt(minus_expm1(2.0 * decay))
        lam8 = jnp.exp(-decay * float(SUB))
        step = [jnp.broadcast_to(lam8[n : n + 1], (SUB, LANES)) for n in range(modes)]
        within = [jnp.exp(-decay[n : n + 1] * ahead) for n in range(modes)]
        kernel = [base[n : n + 1] * within[n] for n in range(modes)]
        for j in range(tiles):
            taps_ref[pl.ds(j * SUB, SUB), :] = sum(kernel)
            if j + 1 < tiles:
                kernel = [kernel[n] * step[n] for n in range(modes)]
        scale = base * jnp.exp(-decay)
        out_ref[2 * rows : 2 * rows + modes, lanes] = decay
        out_ref[2 * rows + modes :, lanes] = scale
        fade = None
        for b in range(count):
            if b:
                entry = scale * blocks_ref[b - 1, :, lanes]
                entry = [entry[n : n + 1] * within[n] for n in range(modes)]
                if fade is None:
                    fade = entry
                else:
                    fade = [fade[n] + entry[n] for n in range(modes)]
            acc = []
            mixed = []
            for j in range(tiles):
                at = pl.ds(b * BLOCK + j * SUB, SUB)
                if fade is None:
                    acc.append(jnp.zeros((SUB, LANES), jnp.float32))
                else:
                    acc.append(sum(fade))
                    fade = [fade[n] * step[n] for n in range(modes)]
                mixed.append(
                    key_ref[at, lanes].astype(jnp.float32)
                    * value_ref[at, lanes].astype(jnp.float32)
                )
            for r in range(SUB):
                if r == 0:
                    moved = mixed
                else:
                    rolled = [pltpu.roll(tile, r, 0) for tile in mixed]
                    moved = []
                    for j in range(tiles):
                        above = rolled[j - 1] if j else jnp.zeros_like(rolled[0])
                        moved.append(jnp.where(sub < r, above, rolled[j]))
                for q in range(tiles):
                    tap = taps_ref[pl.ds(q * SUB + r, 1), :]
                    for j in range(q, tiles):
                        acc[j] = acc[j] + tap * moved[j - q]
            for j in range(tiles):
                row = b * BLOCK + j * SUB
                gate = gate_ref[pl.ds(row, SUB), lanes].astype(jnp.float32)
                out_ref[pl.ds(row, SUB), lanes] = gate * acc[j]
                out_ref[pl.ds(rows + row, SUB), lanes] = gate
        return carry

    lax.fori_loop(0, decay_ref.shape[1] // LANES, lane_group, 0)


def local_conv(blocks, gate, key, value, residues, decay):
    rows, chans = key.shape
    modes = decay.shape[0]
    return pl.pallas_call(
        local_kernel,
        out_shape=jax.ShapeDtypeStruct((2 * (rows + modes), chans), jnp.float32),
        scratch_shapes=[pltpu.VMEM((BLOCK, LANES), jnp.float32)],
        name="local_conv",
    )(blocks, gate, key, value, residues, decay)


def scan_kernel(place_ref, chips_ref, own_ref, decay_ref, out_ref, *, rows):
    lam_chip = jnp.exp(-decay_ref[...] * float(2 * rows))
    before = jnp.zeros_like(lam_chip)
    for j in range(chips_ref.shape[0]):
        before = jnp.where(
            j < place_ref[0], before * lam_chip + chips_ref[j], before
        )
    out_ref[0] = before
    out_ref[1] = own_ref[0]


def chip_scan(place, chips, copies, decay, rows):
    shape = (2,) + decay.shape
    return pl.pallas_call(
        functools.partial(scan_kernel, rows=rows),
        out_shape=jax.ShapeDtypeStruct(shape, jnp.float32),
        grid_spec=pltpu.PrefetchScalarGridSpec(
            num_scalar_prefetch=1,
            grid=(1,),
            in_specs=[whole(chips.shape), whole((1,) + decay.shape), whole(decay.shape)],
            out_specs=whole(shape),
        ),
        cost_estimate=pl.CostEstimate(
            flops=2 * 10**11, transcendentals=0, bytes_accessed=2 * 10**8
        ),
        name="chip_scan",
    )(place, near_core(chips), copies, decay)


def gate_kernel(place_ref, states_ref, own_ref, peer_ref, out_ref):
    modes = states_ref.shape[2]
    chans = own_ref.shape[1]
    rows = out_ref.shape[0]
    core = place_ref[1]
    ahead = sub_iota().astype(jnp.float32)

    for part, pack_ref in enumerate((own_ref, peer_ref)):
        side = place_ref[2] if part == 0 else 1 - place_ref[2]

        def lane_group(g, carry, part=part, pack_ref=pack_ref, side=side):
            start = pl.multiple_of(g * LANES, LANES)
            lanes = pl.ds(start, LANES)
            decay = pack_ref[2 * rows : 2 * rows + modes, lanes]
            scale = pack_ref[2 * rows + modes :, lanes]
            lam_rows = jnp.exp(-decay * float(rows))
            before = states_ref[2 * side, 0, :, lanes] * lam_rows
            before = before + states_ref[2 * side + 1, 0, :, lanes]
            after = before * lam_rows + states_ref[2 * side, 1, :, lanes]
            entry = scale * jnp.where(core == 0, before, after)
            lam8 = jnp.exp(-decay * float(SUB))
            step = [
                jnp.broadcast_to(lam8[n : n + 1], (SUB, LANES)) for n in range(modes)
            ]
            fade = [
                entry[n : n + 1] * jnp.exp(-decay[n : n + 1] * ahead)
                for n in range(modes)
            ]
            target = pl.ds(pl.multiple_of(part * chans + start, LANES), LANES)
            for j in range(0, rows, 2 * SUB):
                tiles = []
                for row in (j, j + SUB):
                    gate = pack_ref[pl.ds(rows + row, SUB), lanes]
                    tiles.append(pack_ref[pl.ds(row, SUB), lanes] + gate * sum(fade))
                    fade = [fade[n] * step[n] for n in range(modes)]
                out_ref[pl.ds(j, 2 * SUB), target] = jnp.concatenate(tiles).astype(
                    jnp.bfloat16
                )
            return carry

        lax.fori_loop(0, chans // LANES, lane_group, 0)


def gated_both(place, states, own, peer, rows):
    chans = own.shape[1]
    args = (states, own, peer)
    return pl.pallas_call(
        gate_kernel,
        out_shape=jax.ShapeDtypeStruct((rows, 2 * chans), jnp.bfloat16),
        grid_spec=pltpu.PrefetchScalarGridSpec(
            num_scalar_prefetch=1,
            grid=(1,),
            in_specs=[whole(a.shape) for a in args],
            out_specs=whole((rows, 2 * chans)),
        ),
        name="gated_both",
    )(place, *args)


def weights_kernel(place_ref, own_ref, near_ref, far_ref, out_ref):
    half = near_ref.shape[0]
    chans = 2 * half
    core = place_ref[1]
    parity = place_ref[3]
    here = pl.ds(pl.multiple_of(chans + core * half, half), half)
    there = pl.ds(pl.multiple_of(chans + (1 - core) * half, half), half)
    for kept in range(2):
        side = parity if kept else 1 - parity
        source = pl.ds(pl.multiple_of(side * chans, chans), chans)
        out_ref[kept, :chans, :] = own_ref[:, source]
        out_ref[kept, here, :] = near_ref[:, source].astype(jnp.bfloat16)
        out_ref[kept, there, :] = far_ref[:, source].astype(jnp.bfloat16)


def joined_weights(place, weight, near, far):
    chans = weight.shape[0]
    half, cols = near.shape
    wide = pl.BlockSpec((half, 2 * chans), lambda i, p: (0, i))
    return pl.pallas_call(
        weights_kernel,
        out_shape=jax.ShapeDtypeStruct((2, 2 * chans, cols // 2), jnp.bfloat16),
        grid_spec=pltpu.PrefetchScalarGridSpec(
            num_scalar_prefetch=1,
            grid=(4,),
            in_specs=[
                pl.BlockSpec((chans, 2 * chans), lambda i, p: (0, 4 * p[2] + i)),
                wide,
                wide,
            ],
            out_specs=pl.BlockSpec((2, 2 * chans, chans), lambda i, p: (0, 0, i)),
        ),
        name="joined_weights",
    )(place, weight, near, far)


def project_kernel(gated_ref, weight_ref, out_ref):
    chans = out_ref.shape[2]
    for h in range(4):
        out_ref[h] = jnp.dot(
            gated_ref[...],
            weight_ref[:, h * chans : (h + 1) * chans],
            preferred_element_type=jnp.float32,
        )


def project(gated, weight, part, name):
    rows, deep = gated.shape
    cols = weight.shape[2]
    return pl.pallas_call(
        project_kernel,
        out_shape=jax.ShapeDtypeStruct((4, rows, cols // 4), jnp.float32),
        grid=(1,),
        in_specs=[
            whole((rows, deep)),
            pl.BlockSpec((None, deep, cols), lambda i: (part, 0, 0)),
        ],
        out_specs=whole((4, rows, cols // 4)),
        name=name,
    )(gated, weight)


def neighbour_routes(count):
    routes = []
    for y in range(count):
        routes.append((2 * y, 2 * (y ^ 1)))
        other = (y + 1) % count if y % 2 else (y - 1) % count
        routes.append((2 * y + 1, 2 * other + 1))
    return routes


def weight_routes():
    routes = []
    for side in range(2):
        for xh in range(2):
            for core in range(2):
                source = 4 * side + 2 * xh + core
                routes.append((source, 4 * (1 - side) + 2 * (xh ^ core) + core))
    return routes


def on_device(gate_stream, key_stream, value_stream, residues, decay_rates, out_weight):
    rows, chans = key_stream.shape
    swap = [(0, 1), (1, 0)]
    chip = lax.axis_index("z") * lax.axis_size("xh") + lax.axis_index("xh")
    core = lax.axis_index("core")
    side = lax.axis_index("xl")
    place = jnp.stack([chip, core, side, lax.axis_index("yl")]).astype(jnp.int32)
    half, cols = chans // 2, out_weight.shape[1] // 2
    sent = lax.dynamic_slice(
        out_weight, (core * half, (1 - side) * cols), (half, cols)
    ).astype(jnp.float32)
    near = lax.ppermute(sent, ("xl", "xh", "core"), weight_routes())
    far = lax.ppermute(near, "core", swap)
    weight = joined_weights(place, out_weight, near, far)

    chips = lax.axis_size("z") * lax.axis_size("xh")
    blocks, copies = local_states(key_stream, value_stream, decay_rates, chips)
    states = lax.all_to_all(copies, ("z", "xh"), split_axis=0, concat_axis=0, tiled=True)
    own = local_conv(
        blocks, gate_stream, key_stream, value_stream, residues, decay_rates
    )
    peer = lax.ppermute(own, "xl", swap)
    scanned = chip_scan(place, states, copies, decay_rates, rows)
    scanned = lax.all_gather(scanned, ("xl", "core"), axis=0)
    gated = gated_both(place, scanned, own, peer, rows)
    leaving = project(gated, weight, 0, "project_leaving")
    arrived = lax.ppermute(leaving, ("yh", "yl", "core"), neighbour_routes(8))
    kept = project(gated, weight, 1, "project_kept")
    parts = lax.all_to_all(kept + arrived, "yh", split_axis=0, concat_axis=0, tiled=True)
    return jnp.sum(parts, axis=0).astype(jnp.bfloat16)


def solution(mesh):
    inner = Mesh(
        mesh.devices.reshape(2, 4, 2, 8, 2, 2), ("xl", "yh", "yl", "z", "xh", "core")
    )
    time = ("z", "xh", "core")
    chan = ("xl", "yh", "yl")
    return jax.shard_map(
        on_device,
        mesh=inner,
        in_specs=(
            P(time, chan),
            P(time, chan),
            P(time, chan),
            P(None, chan),
            P(None, chan),
            P(chan, None),
        ),
        out_specs=P(time, chan),
        check_vma=False,
    )
```

```python
import functools

import jax
import jax.numpy as jnp
from jax import lax
from jax.experimental import pallas as pl
from jax.experimental.pallas import tpu as pltpu
from jax.sharding import Mesh, PartitionSpec as P

BLOCK = 64
LANES = 128
SUB = 8


def near_core(array):
    return pltpu.with_memory_space_constraint(array, pltpu.VMEM)


def whole(shape):
    return pl.BlockSpec(shape, lambda *_: (0,) * len(shape))


def minus_expm1(x):
    series = 1.0 - x / 8.0
    for k in (7.0, 6.0, 5.0, 4.0, 3.0, 2.0):
        series = 1.0 - x / k * series
    return jnp.where(x < 0.5, x * series, 1.0 - jnp.exp(-x))


def sub_iota():
    return lax.broadcasted_iota(jnp.int32, (SUB, LANES), 0)


def state_kernel(key_ref, value_ref, decay_ref, blocks_ref, copies_ref):
    modes = decay_ref.shape[0]
    count = key_ref.shape[0] // BLOCK
    tiles = BLOCK // SUB
    back = (SUB - 1 - sub_iota()).astype(jnp.float32)

    def lane_group(g, carry):
        lanes = pl.ds(pl.multiple_of(g * LANES, LANES), LANES)
        decay = decay_ref[:, lanes]
        lam8 = jnp.exp(-decay * SUB)
        step = [jnp.broadcast_to(lam8[n : n + 1], (SUB, LANES)) for n in range(modes)]
        lam_block = jnp.exp(-decay * BLOCK)
        ends = [jnp.exp(-decay[n : n + 1] * back) for n in range(modes)]
        total = jnp.zeros((modes, LANES), jnp.float32)
        for b in range(count):
            acc = [None] * modes
            for j in range(tiles):
                rows = pl.ds(b * BLOCK + j * SUB, SUB)
                mixed = key_ref[rows, lanes].astype(jnp.float32) * value_ref[
                    rows, lanes
                ].astype(jnp.float32)
                for n in range(modes):
                    acc[n] = mixed if j == 0 else acc[n] * step[n] + mixed
            rows = [
                jnp.sum(acc[n] * ends[n], axis=0, keepdims=True) for n in range(modes)
            ]
            state = jnp.concatenate(rows, axis=0)
            blocks_ref[b, :, lanes] = state
            total = total * lam_block + state
        for j in range(copies_ref.shape[0]):
            copies_ref[j, :, lanes] = total
        return carry

    lax.fori_loop(0, decay_ref.shape[1] // LANES, lane_group, 0)


def local_states(key_stream, value_stream, decay_rates, chips):
    rows, chans = key_stream.shape
    modes = decay_rates.shape[0]
    return pl.pallas_call(
        state_kernel,
        out_shape=(
            jax.ShapeDtypeStruct((rows // BLOCK, modes, chans), jnp.float32),
            jax.ShapeDtypeStruct((chips, modes, chans), jnp.float32),
        ),
        name="local_states",
    )(key_stream, value_stream, decay_rates)


def local_kernel(
    blocks_ref, gate_ref, key_ref, value_ref, residues_ref, decay_ref, out_ref, taps_ref
):
    modes = decay_ref.shape[0]
    rows = key_ref.shape[0]
    count = rows // BLOCK
    tiles = BLOCK // SUB
    sub = sub_iota()
    ahead = sub.astype(jnp.float32)

    def lane_group(g, carry):
        lanes = pl.ds(pl.multiple_of(g * LANES, LANES), LANES)
        decay = decay_ref[:, lanes]
        base = residues_ref[:, lanes] * jnp.sqrt(minus_expm1(2.0 * decay))
        lam8 = jnp.exp(-decay * float(SUB))
        step = [jnp.broadcast_to(lam8[n : n + 1], (SUB, LANES)) for n in range(modes)]
        within = [jnp.exp(-decay[n : n + 1] * ahead) for n in range(modes)]
        kernel = [base[n : n + 1] * within[n] for n in range(modes)]
        for j in range(tiles):
            taps_ref[pl.ds(j * SUB, SUB), :] = sum(kernel)
            if j + 1 < tiles:
                kernel = [kernel[n] * step[n] for n in range(modes)]
        scale = base * jnp.exp(-decay)
        out_ref[2 * rows : 2 * rows + modes, lanes] = decay
        out_ref[2 * rows + modes :, lanes] = scale
        fade = None
        for b in range(count):
            if b:
                entry = scale * blocks_ref[b - 1, :, lanes]
                entry = [entry[n : n + 1] * within[n] for n in range(modes)]
                if fade is None:
                    fade = entry
                else:
                    fade = [fade[n] + entry[n] for n in range(modes)]
            acc = []
            mixed = []
            for j in range(tiles):
                at = pl.ds(b * BLOCK + j * SUB, SUB)
                if fade is None:
                    acc.append(jnp.zeros((SUB, LANES), jnp.float32))
                else:
                    acc.append(sum(fade))
                    fade = [fade[n] * step[n] for n in range(modes)]
                mixed.append(
                    key_ref[at, lanes].astype(jnp.float32)
                    * value_ref[at, lanes].astype(jnp.float32)
                )
            for r in range(SUB):
                if r == 0:
                    moved = mixed
                else:
                    rolled = [pltpu.roll(tile, r, 0) for tile in mixed]
                    moved = []
                    for j in range(tiles):
                        above = rolled[j - 1] if j else jnp.zeros_like(rolled[0])
                        moved.append(jnp.where(sub < r, above, rolled[j]))
                for q in range(tiles):
                    tap = taps_ref[pl.ds(q * SUB + r, 1), :]
                    for j in range(q, tiles):
                        acc[j] = acc[j] + tap * moved[j - q]
            for j in range(tiles):
                row = b * BLOCK + j * SUB
                gate = gate_ref[pl.ds(row, SUB), lanes].astype(jnp.float32)
                out_ref[pl.ds(row, SUB), lanes] = gate * acc[j]
                out_ref[pl.ds(rows + row, SUB), lanes] = gate
        return carry

    lax.fori_loop(0, decay_ref.shape[1] // LANES, lane_group, 0)


def local_conv(blocks, gate, key, value, residues, decay):
    rows, chans = key.shape
    modes = decay.shape[0]
    return pl.pallas_call(
        local_kernel,
        out_shape=jax.ShapeDtypeStruct((2 * (rows + modes), chans), jnp.float32),
        scratch_shapes=[pltpu.VMEM((BLOCK, LANES), jnp.float32)],
        name="local_conv",
    )(blocks, gate, key, value, residues, decay)


def scan_kernel(place_ref, chips_ref, own_ref, decay_ref, out_ref, *, rows):
    lam_chip = jnp.exp(-decay_ref[...] * float(2 * rows))
    before = jnp.zeros_like(lam_chip)
    for j in range(chips_ref.shape[0]):
        before = jnp.where(
            j < place_ref[0], before * lam_chip + chips_ref[j], before
        )
    out_ref[0] = before
    out_ref[1] = own_ref[0]


def chip_scan(place, chips, copies, decay, rows):
    shape = (2,) + decay.shape
    return pl.pallas_call(
        functools.partial(scan_kernel, rows=rows),
        out_shape=jax.ShapeDtypeStruct(shape, jnp.float32),
        grid_spec=pltpu.PrefetchScalarGridSpec(
            num_scalar_prefetch=1,
            grid=(1,),
            in_specs=[whole(chips.shape), whole((1,) + decay.shape), whole(decay.shape)],
            out_specs=whole(shape),
        ),
        cost_estimate=pl.CostEstimate(
            flops=2 * 10**11, transcendentals=0, bytes_accessed=2 * 10**8
        ),
        name="chip_scan",
    )(place, near_core(chips), copies, decay)


def gate_kernel(place_ref, states_ref, own_ref, peer_ref, out_ref):
    modes = states_ref.shape[2]
    chans = own_ref.shape[1]
    rows = out_ref.shape[0]
    core = place_ref[1]
    ahead = sub_iota().astype(jnp.float32)

    for part, pack_ref in enumerate((own_ref, peer_ref)):
        side = place_ref[2] if part == 0 else 1 - place_ref[2]

        def lane_group(g, carry, part=part, pack_ref=pack_ref, side=side):
            start = pl.multiple_of(g * LANES, LANES)
            lanes = pl.ds(start, LANES)
            decay = pack_ref[2 * rows : 2 * rows + modes, lanes]
            scale = pack_ref[2 * rows + modes :, lanes]
            lam_rows = jnp.exp(-decay * float(rows))
            before = states_ref[2 * side, 0, :, lanes] * lam_rows
            before = before + states_ref[2 * side + 1, 0, :, lanes]
            after = before * lam_rows + states_ref[2 * side, 1, :, lanes]
            entry = scale * jnp.where(core == 0, before, after)
            lam8 = jnp.exp(-decay * float(SUB))
            step = [
                jnp.broadcast_to(lam8[n : n + 1], (SUB, LANES)) for n in range(modes)
            ]
            fade = [
                entry[n : n + 1] * jnp.exp(-decay[n : n + 1] * ahead)
                for n in range(modes)
            ]
            target = pl.ds(pl.multiple_of(part * chans + start, LANES), LANES)
            for j in range(0, rows, 2 * SUB):
                tiles = []
                for row in (j, j + SUB):
                    gate = pack_ref[pl.ds(rows + row, SUB), lanes]
                    tiles.append(pack_ref[pl.ds(row, SUB), lanes] + gate * sum(fade))
                    fade = [fade[n] * step[n] for n in range(modes)]
                out_ref[pl.ds(j, 2 * SUB), target] = jnp.concatenate(tiles).astype(
                    jnp.bfloat16
                )
            return carry

        lax.fori_loop(0, chans // LANES, lane_group, 0)


def gated_both(place, states, own, peer, rows):
    chans = own.shape[1]
    args = (near_core(states), near_core(own), near_core(peer))
    return pl.pallas_call(
        gate_kernel,
        out_shape=jax.ShapeDtypeStruct((rows, 2 * chans), jnp.bfloat16),
        grid_spec=pltpu.PrefetchScalarGridSpec(
            num_scalar_prefetch=1,
            grid=(1,),
            in_specs=[whole(a.shape) for a in args],
            out_specs=whole((rows, 2 * chans)),
        ),
        name="gated_both",
    )(place, *args)


def project_kernel(place_ref, gated_ref, *refs):
    *weights, out_ref = refs
    half = weights[1].shape[0]
    chans = 2 * half
    core = place_ref[1]
    here = pl.ds(pl.multiple_of(chans + core * half, half), half)
    there = pl.ds(pl.multiple_of(chans + (1 - core) * half, half), half)

    def product(lhs, rhs):
        return jnp.dot(
            lhs, rhs.astype(jnp.bfloat16), preferred_element_type=jnp.float32
        )

    for h in range(4):
        own_ref, near_ref, far_ref = weights[3 * h : 3 * h + 3]
        out_ref[h] = (
            product(gated_ref[:, :chans], own_ref[...])
            + product(gated_ref[:, here], near_ref[...])
            + product(gated_ref[:, there], far_ref[...])
        )


def project(place, gated, weight, near, far, part, name):
    rows, deep = gated.shape
    chans = deep // 2

    def columns(h):
        def at(p):
            return 2 * h + (p[3] if part else 1 - p[3])

        other = pl.BlockSpec((chans // 2, chans), lambda i, p: (0, at(p)))
        own = pl.BlockSpec((chans, chans), lambda i, p: (0, 8 * p[2] + at(p)))
        return [own, other, other]

    return pl.pallas_call(
        project_kernel,
        out_shape=jax.ShapeDtypeStruct((4, rows, chans), jnp.float32),
        grid_spec=pltpu.PrefetchScalarGridSpec(
            num_scalar_prefetch=1,
            grid=(1,),
            in_specs=[whole((rows, deep))] + sum([columns(h) for h in range(4)], []),
            out_specs=whole((4, rows, chans)),
        ),
        name=name,
    )(place, gated, *[weight, near, far] * 4)


def neighbour_routes(count):
    routes = []
    for y in range(count):
        routes.append((2 * y, 2 * (y ^ 1)))
        other = (y + 1) % count if y % 2 else (y - 1) % count
        routes.append((2 * y + 1, 2 * other + 1))
    return routes


def weight_routes():
    routes = []
    for side in range(2):
        for xh in range(2):
            for core in range(2):
                source = 4 * side + 2 * xh + core
                routes.append((source, 4 * (1 - side) + 2 * (xh ^ core) + core))
    return routes


def on_device(gate_stream, key_stream, value_stream, residues, decay_rates, out_weight):
    rows, chans = key_stream.shape
    swap = [(0, 1), (1, 0)]
    chip = lax.axis_index("z") * lax.axis_size("xh") + lax.axis_index("xh")
    core = lax.axis_index("core")
    side = lax.axis_index("xl")
    place = jnp.stack([chip, core, side, lax.axis_index("yl")]).astype(jnp.int32)
    half, cols = chans // 2, out_weight.shape[1] // 2
    sent = lax.dynamic_slice(
        out_weight, (core * half, (1 - side) * cols), (half, cols)
    ).astype(jnp.float32)
    near = lax.ppermute(sent, ("xl", "xh", "core"), weight_routes())
    far = lax.ppermute(near, "core", swap)

    chips = lax.axis_size("z") * lax.axis_size("xh")
    blocks, copies = local_states(key_stream, value_stream, decay_rates, chips)
    states = lax.all_to_all(copies, ("z", "xh"), split_axis=0, concat_axis=0, tiled=True)
    own = local_conv(
        blocks, gate_stream, key_stream, value_stream, residues, decay_rates
    )
    peer = lax.ppermute(own, "xl", swap)
    scanned = chip_scan(place, states, copies, decay_rates, rows)
    scanned = lax.all_gather(scanned, ("xl", "core"), axis=0)
    gated = gated_both(place, scanned, own, peer, rows)
    leaving = project(place, gated, out_weight, near, far, 0, "project_leaving")
    arrived = lax.ppermute(leaving, ("yh", "yl", "core"), neighbour_routes(8))
    kept = project(place, gated, out_weight, near, far, 1, "project_kept")
    parts = lax.all_to_all(kept + arrived, "yh", split_axis=0, concat_axis=0, tiled=True)
    return jnp.sum(parts, axis=0).astype(jnp.bfloat16)


def solution(mesh):
    inner = Mesh(
        mesh.devices.reshape(2, 4, 2, 8, 2, 2), ("xl", "yh", "yl", "z", "xh", "core")
    )
    time = ("z", "xh", "core")
    chan = ("xl", "yh", "yl")
    return jax.shard_map(
        on_device,
        mesh=inner,
        in_specs=(
            P(time, chan),
            P(time, chan),
            P(time, chan),
            P(None, chan),
            P(None, chan),
            P(chan, None),
        ),
        out_specs=P(time, chan),
        check_vma=False,
    )
```

```python
import functools

import jax
import jax.numpy as jnp
from jax import lax
from jax.experimental import pallas as pl
from jax.experimental.pallas import tpu as pltpu
from jax.sharding import Mesh, PartitionSpec as P

BLOCK = 64
LANES = 128
SUB = 8


def near_core(array):
    return pltpu.with_memory_space_constraint(array, pltpu.VMEM)


def whole(shape):
    return pl.BlockSpec(shape, lambda *_: (0,) * len(shape))


def minus_expm1(x):
    series = 1.0 - x / 8.0
    for k in (7.0, 6.0, 5.0, 4.0, 3.0, 2.0):
        series = 1.0 - x / k * series
    return jnp.where(x < 0.5, x * series, 1.0 - jnp.exp(-x))


def sub_iota():
    return lax.broadcasted_iota(jnp.int32, (SUB, LANES), 0)


def state_kernel(key_ref, value_ref, decay_ref, blocks_ref, copies_ref):
    modes = decay_ref.shape[0]
    count = key_ref.shape[0] // BLOCK
    tiles = BLOCK // SUB
    back = (SUB - 1 - sub_iota()).astype(jnp.float32)

    def lane_group(g, carry):
        lanes = pl.ds(pl.multiple_of(g * LANES, LANES), LANES)
        decay = decay_ref[:, lanes]
        lam8 = jnp.exp(-decay * SUB)
        step = [jnp.broadcast_to(lam8[n : n + 1], (SUB, LANES)) for n in range(modes)]
        lam_block = jnp.exp(-decay * BLOCK)
        ends = [jnp.exp(-decay[n : n + 1] * back) for n in range(modes)]
        total = jnp.zeros((modes, LANES), jnp.float32)
        for b in range(count):
            acc = [None] * modes
            for j in range(tiles):
                rows = pl.ds(b * BLOCK + j * SUB, SUB)
                mixed = key_ref[rows, lanes].astype(jnp.float32) * value_ref[
                    rows, lanes
                ].astype(jnp.float32)
                for n in range(modes):
                    acc[n] = mixed if j == 0 else acc[n] * step[n] + mixed
            rows = [
                jnp.sum(acc[n] * ends[n], axis=0, keepdims=True) for n in range(modes)
            ]
            state = jnp.concatenate(rows, axis=0)
            blocks_ref[b, :, lanes] = state
            total = total * lam_block + state
        for j in range(copies_ref.shape[0]):
            copies_ref[j, :, lanes] = total
        return carry

    lax.fori_loop(0, decay_ref.shape[1] // LANES, lane_group, 0)


def local_states(key_stream, value_stream, decay_rates, chips):
    rows, chans = key_stream.shape
    modes = decay_rates.shape[0]
    return pl.pallas_call(
        state_kernel,
        out_shape=(
            jax.ShapeDtypeStruct((rows // BLOCK, modes, chans), jnp.float32),
            jax.ShapeDtypeStruct((chips, modes, chans), jnp.float32),
        ),
        name="local_states",
    )(key_stream, value_stream, decay_rates)


def local_kernel(
    blocks_ref, gate_ref, key_ref, value_ref, residues_ref, decay_ref, out_ref, taps_ref
):
    modes = decay_ref.shape[0]
    rows = key_ref.shape[0]
    count = rows // BLOCK
    tiles = BLOCK // SUB
    sub = sub_iota()
    ahead = sub.astype(jnp.float32)

    def lane_group(g, carry):
        lanes = pl.ds(pl.multiple_of(g * LANES, LANES), LANES)
        decay = decay_ref[:, lanes]
        base = residues_ref[:, lanes] * jnp.sqrt(minus_expm1(2.0 * decay))
        lam8 = jnp.exp(-decay * float(SUB))
        step = [jnp.broadcast_to(lam8[n : n + 1], (SUB, LANES)) for n in range(modes)]
        within = [jnp.exp(-decay[n : n + 1] * ahead) for n in range(modes)]
        kernel = [base[n : n + 1] * within[n] for n in range(modes)]
        for j in range(tiles):
            taps_ref[pl.ds(j * SUB, SUB), :] = sum(kernel)
            if j + 1 < tiles:
                kernel = [kernel[n] * step[n] for n in range(modes)]
        scale = base * jnp.exp(-decay)
        out_ref[2 * rows : 2 * rows + modes, lanes] = decay
        out_ref[2 * rows + modes :, lanes] = scale
        fade = None
        for b in range(count):
            if b:
                entry = scale * blocks_ref[b - 1, :, lanes]
                entry = [entry[n : n + 1] * within[n] for n in range(modes)]
                if fade is None:
                    fade = entry
                else:
                    fade = [fade[n] + entry[n] for n in range(modes)]
            acc = []
            mixed = []
            for j in range(tiles):
                at = pl.ds(b * BLOCK + j * SUB, SUB)
                if fade is None:
                    acc.append(jnp.zeros((SUB, LANES), jnp.float32))
                else:
                    acc.append(sum(fade))
                    fade = [fade[n] * step[n] for n in range(modes)]
                mixed.append(
                    key_ref[at, lanes].astype(jnp.float32)
                    * value_ref[at, lanes].astype(jnp.float32)
                )
            for r in range(SUB):
                if r == 0:
                    moved = mixed
                else:
                    rolled = [pltpu.roll(tile, r, 0) for tile in mixed]
                    moved = []
                    for j in range(tiles):
                        above = rolled[j - 1] if j else jnp.zeros_like(rolled[0])
                        moved.append(jnp.where(sub < r, above, rolled[j]))
                for q in range(tiles):
                    tap = taps_ref[pl.ds(q * SUB + r, 1), :]
                    for j in range(q, tiles):
                        acc[j] = acc[j] + tap * moved[j - q]
            for j in range(tiles):
                row = b * BLOCK + j * SUB
                gate = gate_ref[pl.ds(row, SUB), lanes].astype(jnp.float32)
                out_ref[pl.ds(row, SUB), lanes] = gate * acc[j]
                out_ref[pl.ds(rows + row, SUB), lanes] = gate
        return carry

    lax.fori_loop(0, decay_ref.shape[1] // LANES, lane_group, 0)


def local_conv(blocks, gate, key, value, residues, decay):
    rows, chans = key.shape
    modes = decay.shape[0]
    return pl.pallas_call(
        local_kernel,
        out_shape=jax.ShapeDtypeStruct((2 * (rows + modes), chans), jnp.float32),
        scratch_shapes=[pltpu.VMEM((BLOCK, LANES), jnp.float32)],
        name="local_conv",
    )(blocks, gate, key, value, residues, decay)


def scan_kernel(place_ref, chips_ref, own_ref, decay_ref, out_ref, *, rows):
    lam_chip = jnp.exp(-decay_ref[...] * float(2 * rows))
    before = jnp.zeros_like(lam_chip)
    for j in range(chips_ref.shape[0]):
        before = jnp.where(
            j < place_ref[0], before * lam_chip + chips_ref[j], before
        )
    out_ref[0] = before
    out_ref[1] = own_ref[0]


def chip_scan(place, chips, copies, decay, rows):
    shape = (2,) + decay.shape
    return pl.pallas_call(
        functools.partial(scan_kernel, rows=rows),
        out_shape=jax.ShapeDtypeStruct(shape, jnp.float32),
        grid_spec=pltpu.PrefetchScalarGridSpec(
            num_scalar_prefetch=1,
            grid=(1,),
            in_specs=[whole(chips.shape), whole((1,) + decay.shape), whole(decay.shape)],
            out_specs=whole(shape),
        ),
        cost_estimate=pl.CostEstimate(
            flops=2 * 10**11, transcendentals=0, bytes_accessed=2 * 10**8
        ),
        name="chip_scan",
    )(place, near_core(chips), copies, decay)


def gate_kernel(place_ref, states_ref, own_ref, peer_ref, out_ref):
    modes = states_ref.shape[2]
    chans = own_ref.shape[1]
    rows = out_ref.shape[0]
    core = place_ref[1]
    ahead = sub_iota().astype(jnp.float32)

    for part, pack_ref in enumerate((own_ref, peer_ref)):
        side = place_ref[2] if part == 0 else 1 - place_ref[2]

        def lane_group(g, carry, part=part, pack_ref=pack_ref, side=side):
            start = pl.multiple_of(g * LANES, LANES)
            lanes = pl.ds(start, LANES)
            decay = pack_ref[2 * rows : 2 * rows + modes, lanes]
            scale = pack_ref[2 * rows + modes :, lanes]
            lam_rows = jnp.exp(-decay * float(rows))
            before = states_ref[2 * side, 0, :, lanes] * lam_rows
            before = before + states_ref[2 * side + 1, 0, :, lanes]
            after = before * lam_rows + states_ref[2 * side, 1, :, lanes]
            entry = scale * jnp.where(core == 0, before, after)
            lam8 = jnp.exp(-decay * float(SUB))
            step = [
                jnp.broadcast_to(lam8[n : n + 1], (SUB, LANES)) for n in range(modes)
            ]
            fade = [
                entry[n : n + 1] * jnp.exp(-decay[n : n + 1] * ahead)
                for n in range(modes)
            ]
            target = pl.ds(pl.multiple_of(part * chans + start, LANES), LANES)
            for j in range(0, rows, 2 * SUB):
                tiles = []
                for row in (j, j + SUB):
                    gate = pack_ref[pl.ds(rows + row, SUB), lanes]
                    tiles.append(pack_ref[pl.ds(row, SUB), lanes] + gate * sum(fade))
                    fade = [fade[n] * step[n] for n in range(modes)]
                out_ref[pl.ds(j, 2 * SUB), target] = jnp.concatenate(tiles).astype(
                    jnp.bfloat16
                )
            return carry

        lax.fori_loop(0, chans // LANES, lane_group, 0)


def gated_both(place, states, own, peer, rows):
    chans = own.shape[1]
    args = (near_core(states), near_core(own), near_core(peer))
    return pl.pallas_call(
        gate_kernel,
        out_shape=jax.ShapeDtypeStruct((rows, 2 * chans), jnp.bfloat16),
        grid_spec=pltpu.PrefetchScalarGridSpec(
            num_scalar_prefetch=1,
            grid=(1,),
            in_specs=[whole(a.shape) for a in args],
            out_specs=whole((rows, 2 * chans)),
        ),
        name="gated_both",
    )(place, *args)


def project_kernel(place_ref, gated_ref, *refs):
    *weights, out_ref = refs
    half = weights[1].shape[0]
    chans = 2 * half
    core = place_ref[1]
    here = pl.ds(pl.multiple_of(chans + core * half, half), half)
    there = pl.ds(pl.multiple_of(chans + (1 - core) * half, half), half)

    def product(lhs, rhs):
        return jnp.dot(
            lhs, rhs.astype(jnp.bfloat16), preferred_element_type=jnp.float32
        )

    for h in range(4):
        own_ref, near_ref, far_ref = weights[3 * h : 3 * h + 3]
        out_ref[h] = (
            product(gated_ref[:, :chans], own_ref[...])
            + product(gated_ref[:, here], near_ref[...])
            + product(gated_ref[:, there], far_ref[...])
        )


def project(place, gated, weight, near, far, part, name):
    rows, deep = gated.shape
    chans = deep // 2

    def columns(h):
        def at(p):
            return 2 * h + (p[3] if part else 1 - p[3])

        other = pl.BlockSpec((chans // 2, chans), lambda i, p: (0, at(p)))
        own = pl.BlockSpec((chans, chans), lambda i, p: (0, 8 * p[2] + at(p)))
        return [own, other, other]

    return pl.pallas_call(
        project_kernel,
        out_shape=pltpu.VMEM(
            (4, rows, chans), jnp.float32
        ),
        grid_spec=pltpu.PrefetchScalarGridSpec(
            num_scalar_prefetch=1,
            grid=(1,),
            in_specs=[whole((rows, deep))] + sum([columns(h) for h in range(4)], []),
            out_specs=whole((4, rows, chans)),
        ),
        name=name,
    )(place, gated, *[weight, near, far] * 4)


def neighbour_routes(count):
    routes = []
    for y in range(count):
        routes.append((2 * y, 2 * (y ^ 1)))
        other = (y + 1) % count if y % 2 else (y - 1) % count
        routes.append((2 * y + 1, 2 * other + 1))
    return routes


def weight_routes():
    routes = []
    for side in range(2):
        for xh in range(2):
            for core in range(2):
                source = 4 * side + 2 * xh + core
                routes.append((source, 4 * (1 - side) + 2 * (xh ^ core) + core))
    return routes


def on_device(gate_stream, key_stream, value_stream, residues, decay_rates, out_weight):
    rows, chans = key_stream.shape
    swap = [(0, 1), (1, 0)]
    chip = lax.axis_index("z") * lax.axis_size("xh") + lax.axis_index("xh")
    core = lax.axis_index("core")
    side = lax.axis_index("xl")
    place = jnp.stack([chip, core, side, lax.axis_index("yl")]).astype(jnp.int32)
    half, cols = chans // 2, out_weight.shape[1] // 2
    sent = lax.dynamic_slice(
        out_weight, (core * half, (1 - side) * cols), (half, cols)
    ).astype(jnp.float32)
    near = lax.ppermute(sent, ("xl", "xh", "core"), weight_routes())
    far = lax.ppermute(near, "core", swap)

    chips = lax.axis_size("z") * lax.axis_size("xh")
    blocks, copies = local_states(key_stream, value_stream, decay_rates, chips)
    states = lax.all_to_all(copies, ("z", "xh"), split_axis=0, concat_axis=0, tiled=True)
    own = local_conv(
        blocks, gate_stream, key_stream, value_stream, residues, decay_rates
    )
    peer = lax.ppermute(own, "xl", swap)
    scanned = chip_scan(place, states, copies, decay_rates, rows)
    scanned = lax.all_gather(scanned, ("xl", "core"), axis=0)
    gated = gated_both(place, scanned, own, peer, rows)
    leaving = project(place, gated, out_weight, near, far, 0, "project_leaving")
    arrived = lax.ppermute(leaving, ("yh", "yl", "core"), neighbour_routes(8))
    kept = project(place, gated, out_weight, near, far, 1, "project_kept")
    total = kept + arrived
    here = lax.axis_index("yh")
    result = lax.dynamic_index_in_dim(total, here, 0, keepdims=False)
    for d in (1, 3, 2):
        block = lax.dynamic_index_in_dim(total, (here + d) & 3, 0, keepdims=False)
        result += lax.ppermute(block, "yh", [(h, (h + d) % 4) for h in range(4)])
    return result.astype(jnp.bfloat16)


def solution(mesh):
    inner = Mesh(
        mesh.devices.reshape(2, 4, 2, 8, 2, 2), ("xl", "yh", "yl", "z", "xh", "core")
    )
    time = ("z", "xh", "core")
    chan = ("xl", "yh", "yl")
    return jax.shard_map(
        on_device,
        mesh=inner,
        in_specs=(
            P(time, chan),
            P(time, chan),
            P(time, chan),
            P(None, chan),
            P(None, chan),
            P(chan, None),
        ),
        out_specs=P(time, chan),
        check_vma=False,
    )
```

```python
import functools

import jax
import jax.numpy as jnp
from jax import lax
from jax.experimental import pallas as pl
from jax.experimental.pallas import tpu as pltpu
from jax.sharding import Mesh, PartitionSpec as P

BLOCK = 64
LANES = 128
SUB = 8


def near_core(array):
    return pltpu.with_memory_space_constraint(array, pltpu.VMEM)


def whole(shape):
    return pl.BlockSpec(shape, lambda *_: (0,) * len(shape))


def minus_expm1(x):
    series = 1.0 - x / 8.0
    for k in (7.0, 6.0, 5.0, 4.0, 3.0, 2.0):
        series = 1.0 - x / k * series
    return jnp.where(x < 0.5, x * series, 1.0 - jnp.exp(-x))


def sub_iota():
    return lax.broadcasted_iota(jnp.int32, (SUB, LANES), 0)


def state_kernel(key_ref, value_ref, decay_ref, blocks_ref, copies_ref):
    modes = decay_ref.shape[0]
    count = key_ref.shape[0] // BLOCK
    tiles = BLOCK // SUB
    back = (SUB - 1 - sub_iota()).astype(jnp.float32)

    def lane_group(g, carry):
        lanes = pl.ds(pl.multiple_of(g * LANES, LANES), LANES)
        decay = decay_ref[:, lanes]
        lam8 = jnp.exp(-decay * SUB)
        step = [jnp.broadcast_to(lam8[n : n + 1], (SUB, LANES)) for n in range(modes)]
        lam_block = jnp.exp(-decay * BLOCK)
        ends = [jnp.exp(-decay[n : n + 1] * back) for n in range(modes)]
        total = jnp.zeros((modes, LANES), jnp.float32)
        for b in range(count):
            acc = [None] * modes
            for j in range(tiles):
                rows = pl.ds(b * BLOCK + j * SUB, SUB)
                mixed = key_ref[rows, lanes].astype(jnp.float32) * value_ref[
                    rows, lanes
                ].astype(jnp.float32)
                for n in range(modes):
                    acc[n] = mixed if j == 0 else acc[n] * step[n] + mixed
            rows = [
                jnp.sum(acc[n] * ends[n], axis=0, keepdims=True) for n in range(modes)
            ]
            state = jnp.concatenate(rows, axis=0)
            blocks_ref[b, :, lanes] = state
            total = total * lam_block + state
        for j in range(copies_ref.shape[0]):
            copies_ref[j, :, lanes] = total
        return carry

    lax.fori_loop(0, decay_ref.shape[1] // LANES, lane_group, 0)


def local_states(key_stream, value_stream, decay_rates, chips):
    rows, chans = key_stream.shape
    modes = decay_rates.shape[0]
    return pl.pallas_call(
        state_kernel,
        out_shape=(
            jax.ShapeDtypeStruct((rows // BLOCK, modes, chans), jnp.float32),
            jax.ShapeDtypeStruct((chips, modes, chans), jnp.float32),
        ),
        name="local_states",
    )(key_stream, value_stream, decay_rates)


def local_kernel(
    blocks_ref, gate_ref, key_ref, value_ref, residues_ref, decay_ref, out_ref, taps_ref
):
    modes = decay_ref.shape[0]
    rows = key_ref.shape[0]
    count = rows // BLOCK
    tiles = BLOCK // SUB
    sub = sub_iota()
    ahead = sub.astype(jnp.float32)

    def lane_group(g, carry):
        lanes = pl.ds(pl.multiple_of(g * LANES, LANES), LANES)
        decay = decay_ref[:, lanes]
        base = residues_ref[:, lanes] * jnp.sqrt(minus_expm1(2.0 * decay))
        lam8 = jnp.exp(-decay * float(SUB))
        step = [jnp.broadcast_to(lam8[n : n + 1], (SUB, LANES)) for n in range(modes)]
        within = [jnp.exp(-decay[n : n + 1] * ahead) for n in range(modes)]
        kernel = [base[n : n + 1] * within[n] for n in range(modes)]
        for j in range(tiles):
            taps_ref[pl.ds(j * SUB, SUB), :] = sum(kernel)
            if j + 1 < tiles:
                kernel = [kernel[n] * step[n] for n in range(modes)]
        scale = base * jnp.exp(-decay)
        out_ref[2 * rows : 2 * rows + modes, lanes] = decay
        out_ref[2 * rows + modes :, lanes] = scale
        fade = None
        for b in range(count):
            if b:
                entry = scale * blocks_ref[b - 1, :, lanes]
                entry = [entry[n : n + 1] * within[n] for n in range(modes)]
                if fade is None:
                    fade = entry
                else:
                    fade = [fade[n] + entry[n] for n in range(modes)]
            acc = []
            mixed = []
            for j in range(tiles):
                at = pl.ds(b * BLOCK + j * SUB, SUB)
                if fade is None:
                    acc.append(jnp.zeros((SUB, LANES), jnp.float32))
                else:
                    acc.append(sum(fade))
                    fade = [fade[n] * step[n] for n in range(modes)]
                mixed.append(
                    key_ref[at, lanes].astype(jnp.float32)
                    * value_ref[at, lanes].astype(jnp.float32)
                )
            for r in range(SUB):
                if r == 0:
                    moved = mixed
                else:
                    rolled = [pltpu.roll(tile, r, 0) for tile in mixed]
                    moved = []
                    for j in range(tiles):
                        above = rolled[j - 1] if j else jnp.zeros_like(rolled[0])
                        moved.append(jnp.where(sub < r, above, rolled[j]))
                for q in range(tiles):
                    tap = taps_ref[pl.ds(q * SUB + r, 1), :]
                    for j in range(q, tiles):
                        acc[j] = acc[j] + tap * moved[j - q]
            for j in range(tiles):
                row = b * BLOCK + j * SUB
                gate = gate_ref[pl.ds(row, SUB), lanes].astype(jnp.float32)
                out_ref[pl.ds(row, SUB), lanes] = gate * acc[j]
                out_ref[pl.ds(rows + row, SUB), lanes] = gate
        return carry

    lax.fori_loop(0, decay_ref.shape[1] // LANES, lane_group, 0)


def local_conv(blocks, gate, key, value, residues, decay):
    rows, chans = key.shape
    modes = decay.shape[0]
    return pl.pallas_call(
        local_kernel,
        out_shape=jax.ShapeDtypeStruct((2 * (rows + modes), chans), jnp.float32),
        scratch_shapes=[pltpu.VMEM((BLOCK, LANES), jnp.float32)],
        name="local_conv",
    )(blocks, gate, key, value, residues, decay)


def scan_kernel(place_ref, chips_ref, own_ref, decay_ref, out_ref, *, rows):
    lam_chip = jnp.exp(-decay_ref[...] * float(2 * rows))
    before = jnp.zeros_like(lam_chip)
    for j in range(chips_ref.shape[0]):
        before = jnp.where(
            j < place_ref[0], before * lam_chip + chips_ref[j], before
        )
    out_ref[0] = before
    out_ref[1] = own_ref[0]


def chip_scan(place, chips, copies, decay, rows):
    shape = (2,) + decay.shape
    return pl.pallas_call(
        functools.partial(scan_kernel, rows=rows),
        out_shape=pltpu.VMEM(shape, jnp.float32),
        grid_spec=pltpu.PrefetchScalarGridSpec(
            num_scalar_prefetch=1,
            grid=(1,),
            in_specs=[whole(chips.shape), whole((1,) + decay.shape), whole(decay.shape)],
            out_specs=whole(shape),
        ),
        cost_estimate=pl.CostEstimate(
            flops=2 * 10**11, transcendentals=0, bytes_accessed=2 * 10**8
        ),
        name="chip_scan",
    )(place, near_core(chips), copies, decay)


def gate_kernel(place_ref, states_ref, own_ref, peer_ref, out_ref):
    modes = states_ref.shape[2]
    chans = own_ref.shape[1]
    rows = out_ref.shape[0]
    core = place_ref[1]
    ahead = sub_iota().astype(jnp.float32)

    for part, pack_ref in enumerate((own_ref, peer_ref)):
        side = place_ref[2] if part == 0 else 1 - place_ref[2]

        def lane_group(g, carry, part=part, pack_ref=pack_ref, side=side):
            start = pl.multiple_of(g * LANES, LANES)
            lanes = pl.ds(start, LANES)
            decay = pack_ref[2 * rows : 2 * rows + modes, lanes]
            scale = pack_ref[2 * rows + modes :, lanes]
            lam_rows = jnp.exp(-decay * float(rows))
            before = states_ref[2 * side, 0, :, lanes] * lam_rows
            before = before + states_ref[2 * side + 1, 0, :, lanes]
            after = before * lam_rows + states_ref[2 * side, 1, :, lanes]
            entry = scale * jnp.where(core == 0, before, after)
            lam8 = jnp.exp(-decay * float(SUB))
            step = [
                jnp.broadcast_to(lam8[n : n + 1], (SUB, LANES)) for n in range(modes)
            ]
            fade = [
                entry[n : n + 1] * jnp.exp(-decay[n : n + 1] * ahead)
                for n in range(modes)
            ]
            target = pl.ds(pl.multiple_of(part * chans + start, LANES), LANES)
            for j in range(0, rows, 2 * SUB):
                tiles = []
                for row in (j, j + SUB):
                    gate = pack_ref[pl.ds(rows + row, SUB), lanes]
                    tiles.append(pack_ref[pl.ds(row, SUB), lanes] + gate * sum(fade))
                    fade = [fade[n] * step[n] for n in range(modes)]
                out_ref[pl.ds(j, 2 * SUB), target] = jnp.concatenate(tiles).astype(
                    jnp.bfloat16
                )
            return carry

        lax.fori_loop(0, chans // LANES, lane_group, 0)


def gated_both(place, states, own, peer, rows):
    chans = own.shape[1]
    args = (near_core(states), near_core(own), near_core(peer))
    return pl.pallas_call(
        gate_kernel,
        out_shape=pltpu.VMEM((rows, 2 * chans), jnp.bfloat16),
        grid_spec=pltpu.PrefetchScalarGridSpec(
            num_scalar_prefetch=1,
            grid=(1,),
            in_specs=[whole(a.shape) for a in args],
            out_specs=whole((rows, 2 * chans)),
        ),
        name="gated_both",
    )(place, *args)


def project_kernel(place_ref, gated_ref, *refs):
    *weights, out_ref = refs
    half = weights[1].shape[0]
    chans = 2 * half
    core = place_ref[1]
    here = pl.ds(pl.multiple_of(chans + core * half, half), half)
    there = pl.ds(pl.multiple_of(chans + (1 - core) * half, half), half)

    def product(lhs, rhs):
        return jnp.dot(
            lhs, rhs.astype(jnp.bfloat16), preferred_element_type=jnp.float32
        )

    for h in range(4):
        own_ref, near_ref, far_ref = weights[3 * h : 3 * h + 3]
        out_ref[h] = (
            product(gated_ref[:, :chans], own_ref[...])
            + product(gated_ref[:, here], near_ref[...])
            + product(gated_ref[:, there], far_ref[...])
        )


def project(place, gated, weight, near, far, part, name):
    rows, deep = gated.shape
    chans = deep // 2

    def columns(h):
        def at(p):
            return 2 * h + (p[3] if part else 1 - p[3])

        other = pl.BlockSpec((chans // 2, chans), lambda i, p: (0, at(p)))
        own = pl.BlockSpec((chans, chans), lambda i, p: (0, 8 * p[2] + at(p)))
        return [own, other, other]

    return pl.pallas_call(
        project_kernel,
        out_shape=pltpu.VMEM(
            (4, rows, chans), jnp.float32
        ),
        grid_spec=pltpu.PrefetchScalarGridSpec(
            num_scalar_prefetch=1,
            grid=(1,),
            in_specs=[whole((rows, deep))] + sum([columns(h) for h in range(4)], []),
            out_specs=whole((4, rows, chans)),
        ),
        name=name,
    )(place, near_core(gated), *[weight, near, far] * 4)


def neighbour_routes(count):
    routes = []
    for y in range(count):
        routes.append((2 * y, 2 * (y ^ 1)))
        other = (y + 1) % count if y % 2 else (y - 1) % count
        routes.append((2 * y + 1, 2 * other + 1))
    return routes


def weight_routes():
    routes = []
    for side in range(2):
        for xh in range(2):
            for core in range(2):
                source = 4 * side + 2 * xh + core
                routes.append((source, 4 * (1 - side) + 2 * (xh ^ core) + core))
    return routes


def on_device(gate_stream, key_stream, value_stream, residues, decay_rates, out_weight):
    rows, chans = key_stream.shape
    swap = [(0, 1), (1, 0)]
    chip = lax.axis_index("z") * lax.axis_size("xh") + lax.axis_index("xh")
    core = lax.axis_index("core")
    side = lax.axis_index("xl")
    place = jnp.stack([chip, core, side, lax.axis_index("yl")]).astype(jnp.int32)
    half, cols = chans // 2, out_weight.shape[1] // 2
    sent = lax.dynamic_slice(
        out_weight, (core * half, (1 - side) * cols), (half, cols)
    ).astype(jnp.float32)
    near = lax.ppermute(sent, ("xl", "xh", "core"), weight_routes())
    far = lax.ppermute(near, "core", swap)

    chips = lax.axis_size("z") * lax.axis_size("xh")
    blocks, copies = local_states(key_stream, value_stream, decay_rates, chips)
    states = lax.all_to_all(copies, ("z", "xh"), split_axis=0, concat_axis=0, tiled=True)
    own = local_conv(
        blocks, gate_stream, key_stream, value_stream, residues, decay_rates
    )
    peer = lax.ppermute(own, "xl", swap)
    scanned = chip_scan(place, states, copies, decay_rates, rows)
    scanned = lax.all_gather(scanned, ("xl", "core"), axis=0)
    gated = gated_both(place, scanned, own, peer, rows)
    leaving = project(place, gated, out_weight, near, far, 0, "project_leaving")
    arrived = lax.ppermute(leaving, ("yh", "yl", "core"), neighbour_routes(8))
    kept = project(place, gated, out_weight, near, far, 1, "project_kept")
    total = kept + arrived
    here = lax.axis_index("yh")
    result = lax.dynamic_index_in_dim(total, here, 0, keepdims=False)
    for d in (1, 3, 2):
        block = lax.dynamic_index_in_dim(total, (here + d) & 3, 0, keepdims=False)
        result += lax.ppermute(block, "yh", [(h, (h + d) % 4) for h in range(4)])
    return result.astype(jnp.bfloat16)


def solution(mesh):
    inner = Mesh(
        mesh.devices.reshape(2, 4, 2, 8, 2, 2), ("xl", "yh", "yl", "z", "xh", "core")
    )
    time = ("z", "xh", "core")
    chan = ("xl", "yh", "yl")
    return jax.shard_map(
        on_device,
        mesh=inner,
        in_specs=(
            P(time, chan),
            P(time, chan),
            P(time, chan),
            P(None, chan),
            P(None, chan),
            P(chan, None),
        ),
        out_specs=P(time, chan),
        check_vma=False,
    )
```

```python
import functools

import jax
import jax.numpy as jnp
from jax import lax
from jax.experimental import pallas as pl
from jax.experimental.pallas import tpu as pltpu
from jax.sharding import Mesh, PartitionSpec as P

BLOCK = 64
LANES = 128
SUB = 8


def near_core(array):
    return pltpu.with_memory_space_constraint(array, pltpu.VMEM)


def whole(shape):
    return pl.BlockSpec(shape, lambda *_: (0,) * len(shape))


def minus_expm1(x):
    series = 1.0 - x / 8.0
    for k in (7.0, 6.0, 5.0, 4.0, 3.0, 2.0):
        series = 1.0 - x / k * series
    return jnp.where(x < 0.5, x * series, 1.0 - jnp.exp(-x))


def tree_sum(terms):
    while len(terms) > 1:
        pairs = [a + b for a, b in zip(terms[::2], terms[1::2])]
        terms = pairs + terms[len(terms) // 2 * 2 :]
    return terms[0]


def sub_iota():
    return lax.broadcasted_iota(jnp.int32, (SUB, LANES), 0)


def state_kernel(key_ref, value_ref, decay_ref, blocks_ref, copies_ref):
    modes = decay_ref.shape[0]
    count = key_ref.shape[0] // BLOCK
    tiles = BLOCK // SUB
    back = (SUB - 1 - sub_iota()).astype(jnp.float32)

    def lane_group(g, carry):
        lanes = pl.ds(pl.multiple_of(g * LANES, LANES), LANES)
        decay = decay_ref[:, lanes]
        lam8 = jnp.exp(-decay * SUB)
        step = [jnp.broadcast_to(lam8[n : n + 1], (SUB, LANES)) for n in range(modes)]
        lam_block = jnp.exp(-decay * BLOCK)
        ends = [jnp.exp(-decay[n : n + 1] * back) for n in range(modes)]
        total = jnp.zeros((modes, LANES), jnp.float32)
        for b in range(count):
            acc = [None] * modes
            for j in range(tiles):
                rows = pl.ds(b * BLOCK + j * SUB, SUB)
                mixed = key_ref[rows, lanes].astype(jnp.float32) * value_ref[
                    rows, lanes
                ].astype(jnp.float32)
                for n in range(modes):
                    acc[n] = mixed if j == 0 else acc[n] * step[n] + mixed
            rows = [
                jnp.sum(acc[n] * ends[n], axis=0, keepdims=True) for n in range(modes)
            ]
            state = jnp.concatenate(rows, axis=0)
            blocks_ref[b, :, lanes] = state
            total = total * lam_block + state
        for j in range(copies_ref.shape[0]):
            copies_ref[j, :, lanes] = total
        return carry

    lax.fori_loop(0, decay_ref.shape[1] // LANES, lane_group, 0)


def local_states(key_stream, value_stream, decay_rates, chips):
    rows, chans = key_stream.shape
    modes = decay_rates.shape[0]
    return pl.pallas_call(
        state_kernel,
        out_shape=(
            jax.ShapeDtypeStruct((rows // BLOCK, modes, chans), jnp.float32),
            jax.ShapeDtypeStruct((chips, modes, chans), jnp.float32),
        ),
        name="local_states",
    )(key_stream, value_stream, decay_rates)


def local_kernel(
    blocks_ref, gate_ref, key_ref, value_ref, residues_ref, decay_ref, out_ref, taps_ref
):
    modes = decay_ref.shape[0]
    rows = key_ref.shape[0]
    count = rows // BLOCK
    tiles = BLOCK // SUB
    sub = sub_iota()
    ahead = sub.astype(jnp.float32)

    def lane_group(g, carry):
        lanes = pl.ds(pl.multiple_of(g * LANES, LANES), LANES)
        decay = decay_ref[:, lanes]
        base = residues_ref[:, lanes] * jnp.sqrt(minus_expm1(2.0 * decay))
        lam8 = jnp.exp(-decay * float(SUB))
        step = [jnp.broadcast_to(lam8[n : n + 1], (SUB, LANES)) for n in range(modes)]
        within = [jnp.exp(-decay[n : n + 1] * ahead) for n in range(modes)]
        kernel = [base[n : n + 1] * within[n] for n in range(modes)]
        for j in range(tiles):
            taps_ref[pl.ds(j * SUB, SUB), :] = tree_sum(kernel)
            if j + 1 < tiles:
                kernel = [kernel[n] * step[n] for n in range(modes)]
        scale = base * jnp.exp(-decay)
        out_ref[2 * rows : 2 * rows + modes, lanes] = decay
        out_ref[2 * rows + modes :, lanes] = scale
        fade = None
        for b in range(count):
            if b:
                entry = scale * blocks_ref[b - 1, :, lanes]
                entry = [entry[n : n + 1] * within[n] for n in range(modes)]
                if fade is None:
                    fade = entry
                else:
                    fade = [fade[n] + entry[n] for n in range(modes)]
            acc = []
            mixed = []
            for j in range(tiles):
                at = pl.ds(b * BLOCK + j * SUB, SUB)
                if fade is None:
                    acc.append(jnp.zeros((SUB, LANES), jnp.float32))
                else:
                    acc.append(tree_sum(fade))
                    fade = [fade[n] * step[n] for n in range(modes)]
                mixed.append(
                    key_ref[at, lanes].astype(jnp.float32)
                    * value_ref[at, lanes].astype(jnp.float32)
                )
            for r in range(SUB):
                if r == 0:
                    moved = mixed
                else:
                    rolled = [pltpu.roll(tile, r, 0) for tile in mixed]
                    moved = []
                    for j in range(tiles):
                        above = rolled[j - 1] if j else jnp.zeros_like(rolled[0])
                        moved.append(jnp.where(sub < r, above, rolled[j]))
                for q in range(tiles):
                    tap = taps_ref[pl.ds(q * SUB + r, 1), :]
                    for j in range(q, tiles):
                        acc[j] = acc[j] + tap * moved[j - q]
            for j in range(tiles):
                row = b * BLOCK + j * SUB
                gate = gate_ref[pl.ds(row, SUB), lanes].astype(jnp.float32)
                out_ref[pl.ds(row, SUB), lanes] = gate * acc[j]
                out_ref[pl.ds(rows + row, SUB), lanes] = gate
        return carry

    lax.fori_loop(0, decay_ref.shape[1] // LANES, lane_group, 0)


def local_conv(blocks, gate, key, value, residues, decay):
    rows, chans = key.shape
    modes = decay.shape[0]
    return pl.pallas_call(
        local_kernel,
        out_shape=jax.ShapeDtypeStruct((2 * (rows + modes), chans), jnp.float32),
        scratch_shapes=[pltpu.VMEM((BLOCK, LANES), jnp.float32)],
        name="local_conv",
    )(blocks, gate, key, value, residues, decay)


def scan_kernel(place_ref, chips_ref, own_ref, decay_ref, out_ref, *, rows):
    lam_chip = jnp.exp(-decay_ref[...] * float(2 * rows))
    before = jnp.zeros_like(lam_chip)
    for j in range(chips_ref.shape[0]):
        before = jnp.where(
            j < place_ref[0], before * lam_chip + chips_ref[j], before
        )
    out_ref[0] = before
    out_ref[1] = own_ref[0]


def chip_scan(place, chips, copies, decay, rows):
    shape = (2,) + decay.shape
    return pl.pallas_call(
        functools.partial(scan_kernel, rows=rows),
        out_shape=pltpu.VMEM(shape, jnp.float32),
        grid_spec=pltpu.PrefetchScalarGridSpec(
            num_scalar_prefetch=1,
            grid=(1,),
            in_specs=[whole(chips.shape), whole((1,) + decay.shape), whole(decay.shape)],
            out_specs=whole(shape),
        ),
        cost_estimate=pl.CostEstimate(
            flops=2 * 10**11, transcendentals=0, bytes_accessed=2 * 10**8
        ),
        name="chip_scan",
    )(place, near_core(chips), copies, decay)


def gate_kernel(place_ref, states_ref, own_ref, peer_ref, out_ref):
    modes = states_ref.shape[2]
    chans = own_ref.shape[1]
    rows = out_ref.shape[0]
    core = place_ref[1]
    ahead = sub_iota().astype(jnp.float32)

    for part, pack_ref in enumerate((own_ref, peer_ref)):
        side = place_ref[2] if part == 0 else 1 - place_ref[2]

        def lane_group(g, carry, part=part, pack_ref=pack_ref, side=side):
            start = pl.multiple_of(g * LANES, LANES)
            lanes = pl.ds(start, LANES)
            decay = pack_ref[2 * rows : 2 * rows + modes, lanes]
            scale = pack_ref[2 * rows + modes :, lanes]
            lam_rows = jnp.exp(-decay * float(rows))
            before = states_ref[2 * side, 0, :, lanes] * lam_rows
            before = before + states_ref[2 * side + 1, 0, :, lanes]
            after = before * lam_rows + states_ref[2 * side, 1, :, lanes]
            entry = scale * jnp.where(core == 0, before, after)
            lam8 = jnp.exp(-decay * float(SUB))
            step = [
                jnp.broadcast_to(lam8[n : n + 1], (SUB, LANES)) for n in range(modes)
            ]
            fade = [
                entry[n : n + 1] * jnp.exp(-decay[n : n + 1] * ahead)
                for n in range(modes)
            ]
            target = pl.ds(pl.multiple_of(part * chans + start, LANES), LANES)
            for j in range(0, rows, 2 * SUB):
                tiles = []
                for row in (j, j + SUB):
                    gate = pack_ref[pl.ds(rows + row, SUB), lanes]
                    tiles.append(pack_ref[pl.ds(row, SUB), lanes] + gate * tree_sum(fade))
                    fade = [fade[n] * step[n] for n in range(modes)]
                out_ref[pl.ds(j, 2 * SUB), target] = jnp.concatenate(tiles).astype(
                    jnp.bfloat16
                )
            return carry

        lax.fori_loop(0, chans // LANES, lane_group, 0)


def gated_both(place, states, own, peer, rows):
    chans = own.shape[1]
    args = (near_core(states), near_core(own), near_core(peer))
    return pl.pallas_call(
        gate_kernel,
        out_shape=pltpu.VMEM((rows, 2 * chans), jnp.bfloat16),
        grid_spec=pltpu.PrefetchScalarGridSpec(
            num_scalar_prefetch=1,
            grid=(1,),
            in_specs=[whole(a.shape) for a in args],
            out_specs=whole((rows, 2 * chans)),
        ),
        name="gated_both",
    )(place, *args)


def project_kernel(place_ref, gated_ref, *refs):
    *weights, out_ref = refs
    half = weights[1].shape[0]
    chans = 2 * half
    core = place_ref[1]
    here = pl.ds(pl.multiple_of(chans + core * half, half), half)
    there = pl.ds(pl.multiple_of(chans + (1 - core) * half, half), half)

    def product(lhs, rhs):
        return jnp.dot(
            lhs, rhs.astype(jnp.bfloat16), preferred_element_type=jnp.float32
        )

    for h in range(4):
        own_ref, near_ref, far_ref = weights[3 * h : 3 * h + 3]
        out_ref[h] = (
            product(gated_ref[:, :chans], own_ref[...])
            + product(gated_ref[:, here], near_ref[...])
            + product(gated_ref[:, there], far_ref[...])
        )


def project(place, gated, weight, near, far, part, name):
    rows, deep = gated.shape
    chans = deep // 2

    def columns(h):
        def at(p):
            return 2 * h + (p[3] if part else 1 - p[3])

        other = pl.BlockSpec((chans // 2, chans), lambda i, p: (0, at(p)))
        own = pl.BlockSpec((chans, chans), lambda i, p: (0, 8 * p[2] + at(p)))
        return [own, other, other]

    return pl.pallas_call(
        project_kernel,
        out_shape=pltpu.VMEM(
            (4, rows, chans), jnp.float32
        ),
        grid_spec=pltpu.PrefetchScalarGridSpec(
            num_scalar_prefetch=1,
            grid=(1,),
            in_specs=[whole((rows, deep))] + sum([columns(h) for h in range(4)], []),
            out_specs=whole((4, rows, chans)),
        ),
        name=name,
    )(place, near_core(gated), *[weight, near, far] * 4)


def neighbour_routes(count):
    routes = []
    for y in range(count):
        routes.append((2 * y, 2 * (y ^ 1)))
        other = (y + 1) % count if y % 2 else (y - 1) % count
        routes.append((2 * y + 1, 2 * other + 1))
    return routes


def weight_routes():
    routes = []
    for side in range(2):
        for xh in range(2):
            for core in range(2):
                source = 4 * side + 2 * xh + core
                routes.append((source, 4 * (1 - side) + 2 * (xh ^ core) + core))
    return routes


def on_device(gate_stream, key_stream, value_stream, residues, decay_rates, out_weight):
    rows, chans = key_stream.shape
    swap = [(0, 1), (1, 0)]
    chip = lax.axis_index("z") * lax.axis_size("xh") + lax.axis_index("xh")
    core = lax.axis_index("core")
    side = lax.axis_index("xl")
    place = jnp.stack([chip, core, side, lax.axis_index("yl")]).astype(jnp.int32)
    half, cols = chans // 2, out_weight.shape[1] // 2
    sent = lax.dynamic_slice(
        out_weight, (core * half, (1 - side) * cols), (half, cols)
    ).astype(jnp.float32)
    near = lax.ppermute(sent, ("xl", "xh", "core"), weight_routes())
    far = lax.ppermute(near, "core", swap)

    chips = lax.axis_size("z") * lax.axis_size("xh")
    blocks, copies = local_states(key_stream, value_stream, decay_rates, chips)
    states = lax.all_to_all(copies, ("z", "xh"), split_axis=0, concat_axis=0, tiled=True)
    own = local_conv(
        blocks, gate_stream, key_stream, value_stream, residues, decay_rates
    )
    peer = lax.ppermute(own, "xl", swap)
    scanned = chip_scan(place, states, copies, decay_rates, rows)
    scanned = lax.all_gather(scanned, ("xl", "core"), axis=0)
    gated = gated_both(place, scanned, own, peer, rows)
    leaving = project(place, gated, out_weight, near, far, 0, "project_leaving")
    arrived = lax.ppermute(leaving, ("yh", "yl", "core"), neighbour_routes(8))
    kept = project(place, gated, out_weight, near, far, 1, "project_kept")
    total = kept + arrived
    here = lax.axis_index("yh")
    result = lax.dynamic_index_in_dim(total, here, 0, keepdims=False)
    for d in (1, 3, 2):
        block = lax.dynamic_index_in_dim(total, (here + d) & 3, 0, keepdims=False)
        result += lax.ppermute(block, "yh", [(h, (h + d) % 4) for h in range(4)])
    return result.astype(jnp.bfloat16)


def solution(mesh):
    inner = Mesh(
        mesh.devices.reshape(2, 4, 2, 8, 2, 2), ("xl", "yh", "yl", "z", "xh", "core")
    )
    time = ("z", "xh", "core")
    chan = ("xl", "yh", "yl")
    return jax.shard_map(
        on_device,
        mesh=inner,
        in_specs=(
            P(time, chan),
            P(time, chan),
            P(time, chan),
            P(None, chan),
            P(None, chan),
            P(chan, None),
        ),
        out_specs=P(time, chan),
        check_vma=False,
    )
```

```python
import functools

import jax
import jax.numpy as jnp
from jax import lax
from jax.experimental import pallas as pl
from jax.experimental.pallas import tpu as pltpu
from jax.sharding import Mesh, PartitionSpec as P

BLOCK = 64
LANES = 128
SUB = 8


def near_core(array):
    return pltpu.with_memory_space_constraint(array, pltpu.VMEM)


def whole(shape):
    return pl.BlockSpec(shape, lambda *_: (0,) * len(shape))


def minus_expm1(x):
    series = 1.0 - x / 8.0
    for k in (7.0, 6.0, 5.0, 4.0, 3.0, 2.0):
        series = 1.0 - x / k * series
    return jnp.where(x < 0.5, x * series, 1.0 - jnp.exp(-x))


def sub_iota():
    return lax.broadcasted_iota(jnp.int32, (SUB, LANES), 0)


def state_kernel(key_ref, value_ref, decay_ref, blocks_ref, copies_ref):
    modes = decay_ref.shape[0]
    count = key_ref.shape[0] // BLOCK
    tiles = BLOCK // SUB
    back = (SUB - 1 - sub_iota()).astype(jnp.float32)

    def lane_group(g, carry):
        lanes = pl.ds(pl.multiple_of(g * LANES, LANES), LANES)
        decay = decay_ref[:, lanes]
        lam8 = jnp.exp(-decay * SUB)
        step = [jnp.broadcast_to(lam8[n : n + 1], (SUB, LANES)) for n in range(modes)]
        lam_block = jnp.exp(-decay * BLOCK)
        ends = [jnp.exp(-decay[n : n + 1] * back) for n in range(modes)]
        total = jnp.zeros((modes, LANES), jnp.float32)
        for b in range(count):
            acc = [None] * modes
            for j in range(tiles):
                rows = pl.ds(b * BLOCK + j * SUB, SUB)
                mixed = key_ref[rows, lanes].astype(jnp.float32) * value_ref[
                    rows, lanes
                ].astype(jnp.float32)
                for n in range(modes):
                    acc[n] = mixed if j == 0 else acc[n] * step[n] + mixed
            rows = [
                jnp.sum(acc[n] * ends[n], axis=0, keepdims=True) for n in range(modes)
            ]
            state = jnp.concatenate(rows, axis=0)
            blocks_ref[b, :, lanes] = state
            total = total * lam_block + state
        for j in range(copies_ref.shape[0]):
            copies_ref[j, :, lanes] = total
        return carry

    lax.fori_loop(0, decay_ref.shape[1] // LANES, lane_group, 0)


def local_states(key_stream, value_stream, decay_rates, chips):
    rows, chans = key_stream.shape
    modes = decay_rates.shape[0]
    return pl.pallas_call(
        state_kernel,
        out_shape=(
            jax.ShapeDtypeStruct((rows // BLOCK, modes, chans), jnp.float32),
            pltpu.VMEM((chips, modes, chans), jnp.float32),
        ),
        name="local_states",
    )(key_stream, value_stream, decay_rates)


def local_kernel(
    blocks_ref, gate_ref, key_ref, value_ref, residues_ref, decay_ref, out_ref, taps_ref
):
    modes = decay_ref.shape[0]
    rows = key_ref.shape[0]
    count = rows // BLOCK
    tiles = BLOCK // SUB
    sub = sub_iota()
    ahead = sub.astype(jnp.float32)

    def lane_group(g, carry):
        lanes = pl.ds(pl.multiple_of(g * LANES, LANES), LANES)
        decay = decay_ref[:, lanes]
        base = residues_ref[:, lanes] * jnp.sqrt(minus_expm1(2.0 * decay))
        lam8 = jnp.exp(-decay * float(SUB))
        step = [jnp.broadcast_to(lam8[n : n + 1], (SUB, LANES)) for n in range(modes)]
        within = [jnp.exp(-decay[n : n + 1] * ahead) for n in range(modes)]
        kernel = [base[n : n + 1] * within[n] for n in range(modes)]
        for j in range(tiles):
            taps_ref[pl.ds(j * SUB, SUB), :] = sum(kernel)
            if j + 1 < tiles:
                kernel = [kernel[n] * step[n] for n in range(modes)]
        scale = base * jnp.exp(-decay)
        out_ref[2 * rows : 2 * rows + modes, lanes] = decay
        out_ref[2 * rows + modes :, lanes] = scale
        fade = None
        for b in range(count):
            if b:
                entry = scale * blocks_ref[b - 1, :, lanes]
                entry = [entry[n : n + 1] * within[n] for n in range(modes)]
                if fade is None:
                    fade = entry
                else:
                    fade = [fade[n] + entry[n] for n in range(modes)]
            acc = []
            mixed = []
            for j in range(tiles):
                at = pl.ds(b * BLOCK + j * SUB, SUB)
                if fade is None:
                    acc.append(jnp.zeros((SUB, LANES), jnp.float32))
                else:
                    acc.append(sum(fade))
                    fade = [fade[n] * step[n] for n in range(modes)]
                mixed.append(
                    key_ref[at, lanes].astype(jnp.float32)
                    * value_ref[at, lanes].astype(jnp.float32)
                )
            for r in range(SUB):
                if r == 0:
                    moved = mixed
                else:
                    rolled = [pltpu.roll(tile, r, 0) for tile in mixed]
                    moved = []
                    for j in range(tiles):
                        above = rolled[j - 1] if j else jnp.zeros_like(rolled[0])
                        moved.append(jnp.where(sub < r, above, rolled[j]))
                for q in range(tiles):
                    tap = taps_ref[pl.ds(q * SUB + r, 1), :]
                    for j in range(q, tiles):
                        acc[j] = acc[j] + tap * moved[j - q]
            for j in range(tiles):
                row = b * BLOCK + j * SUB
                gate = gate_ref[pl.ds(row, SUB), lanes].astype(jnp.float32)
                out_ref[pl.ds(row, SUB), lanes] = gate * acc[j]
                out_ref[pl.ds(rows + row, SUB), lanes] = gate
        return carry

    lax.fori_loop(0, decay_ref.shape[1] // LANES, lane_group, 0)


def local_conv(blocks, gate, key, value, residues, decay):
    rows, chans = key.shape
    modes = decay.shape[0]
    return pl.pallas_call(
        local_kernel,
        out_shape=jax.ShapeDtypeStruct((2 * (rows + modes), chans), jnp.float32),
        scratch_shapes=[pltpu.VMEM((BLOCK, LANES), jnp.float32)],
        name="local_conv",
    )(blocks, gate, key, value, residues, decay)


def scan_kernel(place_ref, chips_ref, own_ref, decay_ref, out_ref, *, rows):
    lam_chip = jnp.exp(-decay_ref[...] * float(2 * rows))
    before = jnp.zeros_like(lam_chip)
    for j in range(chips_ref.shape[0]):
        before = jnp.where(
            j < place_ref[0], before * lam_chip + chips_ref[j], before
        )
    out_ref[0] = before
    out_ref[1] = own_ref[0]


def chip_scan(place, chips, copies, decay, rows):
    shape = (2,) + decay.shape
    return pl.pallas_call(
        functools.partial(scan_kernel, rows=rows),
        out_shape=pltpu.VMEM(shape, jnp.float32),
        grid_spec=pltpu.PrefetchScalarGridSpec(
            num_scalar_prefetch=1,
            grid=(1,),
            in_specs=[whole(chips.shape), whole((1,) + decay.shape), whole(decay.shape)],
            out_specs=whole(shape),
        ),
        cost_estimate=pl.CostEstimate(
            flops=2 * 10**11, transcendentals=0, bytes_accessed=2 * 10**8
        ),
        name="chip_scan",
    )(place, near_core(chips), near_core(copies), decay)


def gate_kernel(place_ref, states_ref, own_ref, peer_ref, out_ref):
    modes = states_ref.shape[2]
    chans = own_ref.shape[1]
    rows = out_ref.shape[0]
    core = place_ref[1]
    ahead = sub_iota().astype(jnp.float32)

    for part, pack_ref in enumerate((own_ref, peer_ref)):
        side = place_ref[2] if part == 0 else 1 - place_ref[2]

        def lane_group(g, carry, part=part, pack_ref=pack_ref, side=side):
            start = pl.multiple_of(g * LANES, LANES)
            lanes = pl.ds(start, LANES)
            decay = pack_ref[2 * rows : 2 * rows + modes, lanes]
            scale = pack_ref[2 * rows + modes :, lanes]
            lam_rows = jnp.exp(-decay * float(rows))
            before = states_ref[2 * side, 0, :, lanes] * lam_rows
            before = before + states_ref[2 * side + 1, 0, :, lanes]
            after = before * lam_rows + states_ref[2 * side, 1, :, lanes]
            entry = scale * jnp.where(core == 0, before, after)
            lam8 = jnp.exp(-decay * float(SUB))
            step = [
                jnp.broadcast_to(lam8[n : n + 1], (SUB, LANES)) for n in range(modes)
            ]
            fade = [
                entry[n : n + 1] * jnp.exp(-decay[n : n + 1] * ahead)
                for n in range(modes)
            ]
            target = pl.ds(pl.multiple_of(part * chans + start, LANES), LANES)
            for j in range(0, rows, 2 * SUB):
                tiles = []
                for row in (j, j + SUB):
                    gate = pack_ref[pl.ds(rows + row, SUB), lanes]
                    tiles.append(pack_ref[pl.ds(row, SUB), lanes] + gate * sum(fade))
                    fade = [fade[n] * step[n] for n in range(modes)]
                out_ref[pl.ds(j, 2 * SUB), target] = jnp.concatenate(tiles).astype(
                    jnp.bfloat16
                )
            return carry

        lax.fori_loop(0, chans // LANES, lane_group, 0)


def gated_both(place, states, own, peer, rows):
    chans = own.shape[1]
    args = (near_core(states), near_core(own), near_core(peer))
    return pl.pallas_call(
        gate_kernel,
        out_shape=pltpu.VMEM((rows, 2 * chans), jnp.bfloat16),
        grid_spec=pltpu.PrefetchScalarGridSpec(
            num_scalar_prefetch=1,
            grid=(1,),
            in_specs=[whole(a.shape) for a in args],
            out_specs=whole((rows, 2 * chans)),
        ),
        name="gated_both",
    )(place, *args)


def project_kernel(place_ref, gated_ref, *refs):
    *weights, out_ref = refs
    half = weights[1].shape[0]
    chans = 2 * half
    core = place_ref[1]
    here = pl.ds(pl.multiple_of(chans + core * half, half), half)
    there = pl.ds(pl.multiple_of(chans + (1 - core) * half, half), half)

    def product(lhs, rhs):
        return jnp.dot(
            lhs, rhs.astype(jnp.bfloat16), preferred_element_type=jnp.float32
        )

    for h in range(4):
        own_ref, near_ref, far_ref = weights[3 * h : 3 * h + 3]
        out_ref[h] = (
            product(gated_ref[:, :chans], own_ref[...])
            + product(gated_ref[:, here], near_ref[...])
            + product(gated_ref[:, there], far_ref[...])
        )


def project(place, gated, weight, near, far, part, name):
    rows, deep = gated.shape
    chans = deep // 2

    def columns(h):
        def at(p):
            return 2 * h + (p[3] if part else 1 - p[3])

        other = pl.BlockSpec((chans // 2, chans), lambda i, p: (0, at(p)))
        own = pl.BlockSpec((chans, chans), lambda i, p: (0, 8 * p[2] + at(p)))
        return [own, other, other]

    return pl.pallas_call(
        project_kernel,
        out_shape=pltpu.VMEM(
            (4, rows, chans), jnp.float32
        ),
        grid_spec=pltpu.PrefetchScalarGridSpec(
            num_scalar_prefetch=1,
            grid=(1,),
            in_specs=[whole((rows, deep))] + sum([columns(h) for h in range(4)], []),
            out_specs=whole((4, rows, chans)),
        ),
        name=name,
    )(place, near_core(gated), *[weight, near, far] * 4)


def neighbour_routes(count):
    routes = []
    for y in range(count):
        routes.append((2 * y, 2 * (y ^ 1)))
        other = (y + 1) % count if y % 2 else (y - 1) % count
        routes.append((2 * y + 1, 2 * other + 1))
    return routes


def weight_routes():
    routes = []
    for side in range(2):
        for xh in range(2):
            for core in range(2):
                source = 4 * side + 2 * xh + core
                routes.append((source, 4 * (1 - side) + 2 * (xh ^ core) + core))
    return routes


def on_device(gate_stream, key_stream, value_stream, residues, decay_rates, out_weight):
    rows, chans = key_stream.shape
    swap = [(0, 1), (1, 0)]
    chip = lax.axis_index("z") * lax.axis_size("xh") + lax.axis_index("xh")
    core = lax.axis_index("core")
    side = lax.axis_index("xl")
    place = jnp.stack([chip, core, side, lax.axis_index("yl")]).astype(jnp.int32)
    half, cols = chans // 2, out_weight.shape[1] // 2
    sent = lax.dynamic_slice(
        out_weight, (core * half, (1 - side) * cols), (half, cols)
    ).astype(jnp.float32)
    near = lax.ppermute(sent, ("xl", "xh", "core"), weight_routes())
    far = lax.ppermute(near, "core", swap)

    chips = lax.axis_size("z") * lax.axis_size("xh")
    blocks, copies = local_states(key_stream, value_stream, decay_rates, chips)
    states = lax.all_to_all(copies, ("z", "xh"), split_axis=0, concat_axis=0, tiled=True)
    own = local_conv(
        blocks, gate_stream, key_stream, value_stream, residues, decay_rates
    )
    peer = lax.ppermute(own, "xl", swap)
    scanned = chip_scan(place, states, copies, decay_rates, rows)
    scanned = lax.all_gather(scanned, ("xl", "core"), axis=0)
    gated = gated_both(place, scanned, own, peer, rows)
    leaving = project(place, gated, out_weight, near, far, 0, "project_leaving")
    arrived = lax.ppermute(leaving, ("yh", "yl", "core"), neighbour_routes(8))
    kept = project(place, gated, out_weight, near, far, 1, "project_kept")
    total = kept + arrived
    here = lax.axis_index("yh")
    result = lax.dynamic_index_in_dim(total, here, 0, keepdims=False)
    for d in (1, 3, 2):
        block = lax.dynamic_index_in_dim(total, (here + d) & 3, 0, keepdims=False)
        result += lax.ppermute(block, "yh", [(h, (h + d) % 4) for h in range(4)])
    return result.astype(jnp.bfloat16)


def solution(mesh):
    inner = Mesh(
        mesh.devices.reshape(2, 4, 2, 8, 2, 2), ("xl", "yh", "yl", "z", "xh", "core")
    )
    time = ("z", "xh", "core")
    chan = ("xl", "yh", "yl")
    return jax.shard_map(
        on_device,
        mesh=inner,
        in_specs=(
            P(time, chan),
            P(time, chan),
            P(time, chan),
            P(None, chan),
            P(None, chan),
            P(chan, None),
        ),
        out_specs=P(time, chan),
        check_vma=False,
    )
```
